32 devices in a mesh: groups: 2 (over y), tm: 4 (over z), param: 4 (over x, core).
Axes of the slice: x: 2, y: 2, z: 4, core: 2. Of those that a mesh axis runs over, the one named last changes fastest.
Arguments:
- design: float32 [3, 512, 40960], P(None, ('groups', 'tm'), 'param'), parts along dimension 1, may hold values from -0.03125 to 0.03125
- filter_taps: float32 [3, 512], replicated, may hold values from -0.25 to 0.25
- probes: float32 [40960, 256], P('param', ('groups', 'tm')), parts along dimension 1, may hold values from -6 to 6
Outputs:
- normal_product: float32 [40960, 256], P('param', ('groups', 'tm')), parts along dimension 1
The draws below stay inside these ranges and needn't reach their ends.
There are 2 independent parts, one for each index of `groups`. The reference program is written for one: setup_inputs(seed, part) draws one part's arguments, and reference() takes and returns one part's arrays. A program takes and returns all parts, laid end to end along the dimension named above; an argument that names none is the same for every part. Nothing has to cross between parts.
All inputs are finite; a program needn't handle non-finite values.
Results may differ from the reference program's by a relative error of at most 0.000071.
Values sent between devices are 32-bit elements; how exact they have to be, the bound alone decides.
No kernel may reach another device: no remote copies, remote signals or barrier semaphores. Data moves between devices by JAX's collectives and lax.ppermute only.
A program may use at most 128 MiB of HBM per device.

```python
import jax
import jax.numpy as jnp
from jax import lax

P_SIZE = 40960
COMP = 3
TAPS = 512
PROBES = 128
EPOCHS = 256


def block_levels(key, extent, cuts, least, largest):
    level = 1.0
    for axis_at, parts in cuts:
        draws = jax.random.uniform(jax.random.fold_in(jax.random.fold_in(key, 6), axis_at), (parts,), jnp.float32, least / len(cuts), largest / len(cuts))
        level = level * jnp.repeat(jnp.exp(draws), extent[axis_at] // parts).reshape((-1,) + (1,) * (len(extent) - 1 - axis_at))
    return level


def scatter_about(key, shape, scale, limit, split=(), dtype=jnp.bfloat16):
    values = jax.random.normal(key, shape, jnp.float32) * scale
    if len(split) > 0:
        values = block_levels(key, shape, split, -0.22, 0.18) * values
    return jnp.clip(values, min=-limit, max=limit).astype(dtype)


def setup_inputs(seed: int = 0, part: int = 0) -> dict:
    keys = jax.random.split(jax.random.key(seed), 4)
    own_keys = jax.random.split(jax.random.fold_in(keys[3], part), 4)
    return {
        "design": scatter_about(own_keys[0], (COMP, EPOCHS, P_SIZE), P_SIZE ** -0.5, 0.03125, ((1, 4), (2, 4)), jnp.float32),
        "filter_taps": scatter_about(keys[1], (COMP, TAPS), TAPS ** -0.5, 0.25, (), jnp.float32),
        "probes": scatter_about(own_keys[2], (P_SIZE, PROBES), 1.0, 6.0, ((0, 4), (1, 4)), jnp.float32),
    }


def reference(design, filter_taps, probes):
    highest = lax.Precision.HIGHEST
    projected = jnp.einsum('ctp,pk->ctk', design, probes, precision=highest)
    padding = jnp.zeros((COMP, TAPS - 1, PROBES), jnp.float32)
    padded = jnp.concatenate([padding, projected], axis=1)

    def forward(lag_step, running):
        segment = lax.dynamic_slice_in_dim(padded, TAPS - 1 - lag_step, EPOCHS, 1)
        coefficient = lax.dynamic_slice_in_dim(filter_taps, lag_step, 1, 1)
        return running + coefficient[:, :, None] * segment

    filtered = lax.fori_loop(0, TAPS, forward, jnp.zeros((COMP, EPOCHS, PROBES), jnp.float32))
    padded_after = jnp.concatenate([filtered, padding], axis=1)

    def backward(lag_step, running):
        segment = lax.dynamic_slice_in_dim(padded_after, lag_step, EPOCHS, 1)
        coefficient = lax.dynamic_slice_in_dim(filter_taps, lag_step, 1, 1)
        return running + coefficient[:, :, None] * segment

    weighted = lax.fori_loop(0, TAPS, backward, jnp.zeros((COMP, EPOCHS, PROBES), jnp.float32))
    return jnp.einsum('ctp,ctk->pk', design, weighted, precision=highest)
```

```python
import jax
import jax.numpy as jnp
from jax import lax
from jax.experimental import pallas as pl
from jax.experimental.pallas import tpu as pltpu
from jax.sharding import PartitionSpec as P

HIGHEST = lax.Precision.HIGHEST
HIGH = lax.Precision.HIGH


def normal_rows(filter_taps, block_index, epochs, total):
    components, tap_count = filter_taps.shape
    lanes = -(-(total + tap_count) // 128) * 128
    pad = jnp.zeros((components, lanes - tap_count), jnp.float32)
    ascending = jnp.concatenate([filter_taps, pad], axis=1)[:, None, :]
    descending = jnp.concatenate([filter_taps[:, ::-1], pad], axis=1)[:, None, :]

    def kernel(index_ref, ascending_ref, descending_ref, out_ref, forward_ref):
        rising = jnp.broadcast_to(ascending_ref[0], (epochs, lanes))
        falling = jnp.broadcast_to(descending_ref[0], (epochs, lanes))
        for block in range(total // epochs):
            shift = (block * epochs - (tap_count - 1)) % lanes
            rolled = pltpu.roll(falling, shift, 1, stride=1, stride_axis=0)
            forward_ref[block * epochs : (block + 1) * epochs, :] = rolled[:, :total]
        staggered = pltpu.roll(rising, 0, 1, stride=1, stride_axis=0)
        backward = pltpu.roll(staggered, index_ref[0] * epochs, 1)[:, :total]
        out_ref[0] = jnp.dot(backward, forward_ref[...], precision=HIGHEST, preferred_element_type=jnp.float32)

    return pl.pallas_call(
        kernel,
        grid_spec=pltpu.PrefetchScalarGridSpec(
            num_scalar_prefetch=1,
            grid=(components,),
            in_specs=[
                pl.BlockSpec((1, 1, lanes), lambda c, index: (c, 0, 0)),
                pl.BlockSpec((1, 1, lanes), lambda c, index: (c, 0, 0)),
            ],
            out_specs=pl.BlockSpec((1, epochs, total), lambda c, index: (c, 0, 0)),
            scratch_shapes=[pltpu.VMEM((total, total), jnp.float32)],
        ),
        out_shape=jax.ShapeDtypeStruct((components, epochs, total), jnp.float32),
        name="normal_rows",
    )(jnp.reshape(block_index, (1,)).astype(jnp.int32), ascending, descending)


def body(design, filter_taps, probes):
    components, epochs, coefficients = design.shape
    blocks = lax.axis_size("tm")
    total = blocks * epochs
    rows = normal_rows(filter_taps, lax.axis_index("tm"), epochs, total)
    columns = lax.all_gather(probes.T, "tm", axis=0, tiled=True)
    flat = design.reshape(components * epochs, coefficients)
    partial = lax.dot_general(flat, columns, (((1,), (1,)), ((), ())), precision=HIGH)
    shares = lax.all_gather(partial, "param", axis=0)
    projected = jnp.sum(shares, axis=0).reshape(components, epochs, -1)
    everything = lax.all_gather(projected, "tm", axis=1, tiled=True)
    weighted = jnp.einsum("cts,csk->ctk", rows, everything, precision=HIGHEST)
    weighted = weighted.reshape(components * epochs, -1)
    product = lax.dot_general(weighted, flat, (((0,), (0,)), ((), ())), precision=HIGH)
    result = lax.psum_scatter(product, "tm", scatter_dimension=0, tiled=True)
    return result.T


def solution(mesh):
    in_specs = (P(None, ("groups", "tm"), "param"), P(), P("param", ("groups", "tm")))
    out_specs = P("param", ("groups", "tm"))
    return jax.shard_map(body, mesh=mesh, in_specs=in_specs, out_specs=out_specs, check_vma=False)
```

```python
import math

import jax
import jax.numpy as jnp
from jax import lax
from jax.experimental import pallas as pl
from jax.experimental.pallas import tpu as pltpu
from jax.sharding import PartitionSpec as P

HIGHEST = lax.Precision.HIGHEST
ALONG = (((1,), (1,)), ((), ()))
ACROSS = (((1,), (0,)), ((), ()))


def split(value):
    high = value.astype(jnp.bfloat16)
    return high, (value - high.astype(jnp.float32)).astype(jnp.bfloat16)


def three_passes(left, right, dimensions):
    left_high, left_low = split(left)
    right_high, right_low = split(right)
    height = left.shape[0]
    both = jnp.concatenate([left_high, left_low], axis=0)
    first = lax.dot_general(both, right_high, dimensions, preferred_element_type=jnp.float32)
    last = lax.dot_general(left_high, right_low, dimensions, preferred_element_type=jnp.float32)
    return first[:height] + (first[height:] + last)


def normal_rows(filter_taps, block_index, epochs, total):
    components, tap_count = filter_taps.shape
    lanes = -(-(total + tap_count) // 128) * 128
    pad = jnp.zeros((components, lanes - tap_count), jnp.float32)
    ascending = jnp.concatenate([filter_taps, pad], axis=1)[:, None, :]
    descending = jnp.concatenate([filter_taps[:, ::-1], pad], axis=1)[:, None, :]

    def kernel(index_ref, ascending_ref, descending_ref, out_ref, forward_ref):
        rising = jnp.broadcast_to(ascending_ref[0], (epochs, lanes))
        falling = jnp.broadcast_to(descending_ref[0], (epochs, lanes))
        for block in range(total // epochs):
            shift = (block * epochs - (tap_count - 1)) % lanes
            rolled = pltpu.roll(falling, shift, 1, stride=1, stride_axis=0)
            forward_ref[block * epochs : (block + 1) * epochs, :] = rolled[:, :total]
        staggered = pltpu.roll(rising, 0, 1, stride=1, stride_axis=0)
        backward = pltpu.roll(staggered, index_ref[0] * epochs, 1)[:, :total]
        out_ref[0] = jnp.dot(backward, forward_ref[...], precision=HIGHEST, preferred_element_type=jnp.float32)

    return pl.pallas_call(
        kernel,
        grid_spec=pltpu.PrefetchScalarGridSpec(
            num_scalar_prefetch=1,
            grid=(components,),
            in_specs=[
                pl.BlockSpec((1, 1, lanes), lambda c, index: (c, 0, 0)),
                pl.BlockSpec((1, 1, lanes), lambda c, index: (c, 0, 0)),
            ],
            out_specs=pl.BlockSpec((1, epochs, total), lambda c, index: (c, 0, 0)),
            scratch_shapes=[pltpu.VMEM((total, total), jnp.float32)],
        ),
        out_shape=jax.ShapeDtypeStruct((components, epochs, total), jnp.float32),
        name="normal_rows",
    )(jnp.reshape(block_index, (1,)).astype(jnp.int32), ascending, descending)


def project(design, own, chunk, arrivals, shards):
    components, epochs, coefficients = design.shape
    samples = components * epochs
    slots = len(arrivals) + 1
    rows = arrivals[0][0].shape[0]
    width = math.gcd(coefficients, 2048)
    counts = [len(pieces) for pieces in arrivals]
    pieces = [piece for group in arrivals for piece in group]

    def kernel(shard_ref, design_ref, own_ref, *refs):
        *piece_refs, out_ref = refs
        values = [own_ref[...]]
        start = 0
        for count in counts:
            value = piece_refs[start][...]
            for ref in piece_refs[start + 1 : start + count]:
                value = value + ref[...]
            values.append(value)
            start += count
        block = design_ref[...].reshape(samples, width)
        part = three_passes(jnp.concatenate(values, axis=0), block, ALONG)

        @pl.when(pl.program_id(0) == 0)
        def _():
            out_ref[...] = jnp.zeros_like(out_ref)

        for slot in range(slots):
            out_ref[shard_ref[slot]] += part[slot * rows : (slot + 1) * rows]

    return pl.pallas_call(
        kernel,
        grid_spec=pltpu.PrefetchScalarGridSpec(
            num_scalar_prefetch=1,
            grid=(coefficients // width,),
            in_specs=[
                pl.BlockSpec((components, epochs, width), lambda p, shard: (0, 0, p)),
                pl.BlockSpec((rows, width), lambda p, shard: (chunk, p)),
            ]
            + [pl.BlockSpec((rows, width), lambda p, shard: (0, p)) for _ in pieces],
            out_specs=pl.BlockSpec((slots, rows, samples), lambda p, shard: (0, 0, 0)),
        ),
        out_shape=jax.ShapeDtypeStruct((slots, rows, samples), jnp.float32),
        name="project",
    )(shards, design, own, *pieces)


def multiply(design, taps, everything, shards):
    components, epochs, coefficients = design.shape
    samples = components * epochs
    blocks, slots, rows, _ = everything.shape
    width = math.gcd(coefficients, 2048)

    def kernel(shard_ref, design_ref, taps_ref, everything_ref, *refs):
        *out_refs, weighted_ref = refs

        @pl.when(pl.program_id(0) == 0)
        def _():
            sums = [0.0] * components
            for source in range(blocks):
                block = everything_ref[source].reshape(slots * rows, samples)
                for c in range(components):
                    piece = block[:, c * epochs : (c + 1) * epochs]
                    factor = taps_ref[c, :, source * epochs : (source + 1) * epochs]
                    sums[c] = sums[c] + lax.dot_general(
                        piece, factor, ALONG, precision=HIGHEST, preferred_element_type=jnp.float32
                    )
            weighted_ref[...] = jnp.concatenate(sums, axis=1).reshape(slots, rows, samples)

        weighted = jnp.concatenate([weighted_ref[shard_ref[slot]] for slot in range(slots)], axis=0)
        block = design_ref[...].reshape(samples, width)
        product = three_passes(weighted, block, ACROSS)
        for slot in range(slots):
            out_refs[slot][...] = product[slot * rows : (slot + 1) * rows]

    return pl.pallas_call(
        kernel,
        grid_spec=pltpu.PrefetchScalarGridSpec(
            num_scalar_prefetch=1,
            grid=(coefficients // width,),
            in_specs=[
                pl.BlockSpec((components, epochs, width), lambda p, shard: (0, 0, p)),
                pl.BlockSpec(taps.shape, lambda p, shard: (0, 0, 0)),
                pl.BlockSpec(everything.shape, lambda p, shard: (0, 0, 0, 0)),
            ],
            out_specs=[pl.BlockSpec((rows, width), lambda p, shard: (0, p)) for _ in range(slots)],
            scratch_shapes=[pltpu.VMEM((slots, rows, samples), jnp.float32)],
        ),
        out_shape=[jax.ShapeDtypeStruct((rows, coefficients), jnp.float32) for _ in range(slots)],
        name="multiply",
    )(shards, design, taps, everything)


def step_pairs(length, step, parity):
    pairs = []
    for low in range(parity, length - 1, 2):
        if low - step + 1 >= 0:
            pairs.append((low, low + 1))
        if low + step < length:
            pairs.append((low + 1, low))
    return pairs


def gather_along(value, length):
    arrived = {(0, 0): value, (1, 0): value}
    for step in range(1, length):
        for parity in (0, 1):
            pairs = step_pairs(length, step, parity)
            source = arrived.get((1 - parity, step - 1))
            if pairs:
                arrived[parity, step] = lax.ppermute(source, "tm", pairs)
    return [
        [arrived[key] for key in ((0, slot), (1, length - slot)) if key in arrived] for slot in range(1, length)
    ]


def reduce_along(slots, length):
    pending = {}
    for step in range(length - 1, 0, -1):
        for parity in (0, 1):
            pairs = step_pairs(length, step, parity)
            if pairs:
                value = slots[step] if parity == 0 else slots[length - step]
                if (1 - parity, step + 1) in pending:
                    value = value + pending[1 - parity, step + 1]
                pending[parity, step] = lax.ppermute(value, "tm", [(b, a) for a, b in pairs])
    result = slots[0]
    for parity in (0, 1):
        if (parity, 1) in pending:
            result = result + pending[parity, 1]
    return result


def body(design, filter_taps, probes):
    components, epochs, coefficients = design.shape
    length = lax.axis_size("tm")
    place = lax.axis_index("tm")
    own = probes.T
    columns = own.shape[0]
    chunks = 2 if columns % 16 == 0 else 1
    rows = columns // chunks
    direction = 1 - 2 * (place % 2)
    shards = (place + direction * jnp.arange(length, dtype=jnp.int32)) % length
    taps = normal_rows(filter_taps, place, epochs, length * epochs)
    results = []
    for chunk in range(chunks):
        arrivals = gather_along(own[chunk * rows : (chunk + 1) * rows], length)
        partial = project(design, own, chunk, arrivals, shards)
        projected = jnp.sum(lax.all_gather(partial, "param", axis=0), axis=0)
        everything = lax.all_gather(projected, "tm", axis=0)
        slots = multiply(design, taps, everything, shards)
        results.append(reduce_along(slots, length))
    return jnp.concatenate(results, axis=0).T


def solution(mesh):
    in_specs = (P(None, ("groups", "tm"), "param"), P(), P("param", ("groups", "tm")))
    out_specs = P("param", ("groups", "tm"))
    return jax.shard_map(body, mesh=mesh, in_specs=in_specs, out_specs=out_specs, check_vma=False)
```

```python
import math

import jax
import jax.numpy as jnp
from jax import lax
from jax.experimental import pallas as pl
from jax.experimental.pallas import tpu as pltpu
from jax.sharding import PartitionSpec as P

HIGHEST = lax.Precision.HIGHEST
ALONG = (((1,), (1,)), ((), ()))
ACROSS = (((1,), (0,)), ((), ()))


def split(value):
    high = value.astype(jnp.bfloat16)
    return high, (value - high.astype(jnp.float32)).astype(jnp.bfloat16)


def three_passes(left, right_high, right_low):
    left_high, left_low = split(left)
    height = left.shape[0]
    both = jnp.concatenate([left_high, left_low], axis=0)
    first = lax.dot_general(both, right_high, ACROSS, preferred_element_type=jnp.float32)
    last = lax.dot_general(left_high, right_low, ACROSS, preferred_element_type=jnp.float32)
    return first[:height] + (first[height:] + last)


def split_design(design):
    components, epochs, coefficients = design.shape
    samples = components * epochs
    width = math.gcd(coefficients, 2048)

    def kernel(design_ref, high_ref, low_ref, tall_high_ref, tall_low_ref):
        block = design_ref[...].reshape(samples, width)
        high_ref[...], low_ref[...] = split(block)
        tall_high_ref[...], tall_low_ref[...] = split(block.T)

    flat = jax.ShapeDtypeStruct((samples, coefficients), jnp.bfloat16)
    tall = jax.ShapeDtypeStruct((coefficients, samples), jnp.bfloat16)
    return pl.pallas_call(
        kernel,
        grid=(coefficients // width,),
        in_specs=[pl.BlockSpec((components, epochs, width), lambda p: (0, 0, p))],
        out_specs=[pl.BlockSpec((samples, width), lambda p: (0, p))] * 2
        + [pl.BlockSpec((width, samples), lambda p: (p, 0))] * 2,
        out_shape=[flat, flat, tall, tall],
        compiler_params=pltpu.CompilerParams(vmem_limit_bytes=16 << 20),
        name="split_design",
    )(design)


def normal_rows(filter_taps, block_index, epochs, total):
    components, tap_count = filter_taps.shape
    lanes = -(-(total + tap_count) // 128) * 128
    pad = jnp.zeros((components, lanes - tap_count), jnp.float32)
    ascending = jnp.concatenate([filter_taps, pad], axis=1)[:, None, :]
    descending = jnp.concatenate([filter_taps[:, ::-1], pad], axis=1)[:, None, :]

    def kernel(index_ref, ascending_ref, descending_ref, out_ref, forward_ref):
        rising = jnp.broadcast_to(ascending_ref[0], (epochs, lanes))
        falling = jnp.broadcast_to(descending_ref[0], (epochs, lanes))
        for block in range(total // epochs):
            shift = (block * epochs - (tap_count - 1)) % lanes
            rolled = pltpu.roll(falling, shift, 1, stride=1, stride_axis=0)
            forward_ref[block * epochs : (block + 1) * epochs, :] = rolled[:, :total]
        staggered = pltpu.roll(rising, 0, 1, stride=1, stride_axis=0)
        backward = pltpu.roll(staggered, index_ref[0] * epochs, 1)[:, :total]
        rows = jnp.dot(backward, forward_ref[...], precision=HIGHEST, preferred_element_type=jnp.float32)
        for block in range(total // epochs):
            out_ref[block, 0] = rows[:, block * epochs : (block + 1) * epochs]

    return pl.pallas_call(
        kernel,
        grid_spec=pltpu.PrefetchScalarGridSpec(
            num_scalar_prefetch=1,
            grid=(components,),
            in_specs=[
                pl.BlockSpec((1, 1, lanes), lambda c, index: (c, 0, 0)),
                pl.BlockSpec((1, 1, lanes), lambda c, index: (c, 0, 0)),
            ],
            out_specs=pl.BlockSpec((total // epochs, 1, epochs, epochs), lambda c, index: (0, c, 0, 0)),
            scratch_shapes=[pltpu.VMEM((total, total), jnp.float32)],
        ),
        out_shape=jax.ShapeDtypeStruct((total // epochs, components, epochs, epochs), jnp.float32),
        compiler_params=pltpu.CompilerParams(vmem_limit_bytes=(4 << 20) + 4 * total * total),
        name="normal_rows",
    )(jnp.reshape(block_index, (1,)).astype(jnp.int32), ascending, descending)


def project(tall_high, tall_low, own, chunk, arrivals, shards):
    coefficients, samples = tall_high.shape
    slots = len(arrivals) + 1
    rows = arrivals[0][0].shape[0]
    width = math.gcd(coefficients, 5120)
    counts = [len(pieces) for pieces in arrivals]
    pieces = [piece for group in arrivals for piece in group]

    def kernel(shard_ref, high_ref, low_ref, own_ref, *refs):
        *piece_refs, out_ref = refs
        values = [own_ref[...]]
        start = 0
        for count in counts:
            value = piece_refs[start][...]
            for ref in piece_refs[start + 1 : start + count]:
                value = value + ref[...]
            values.append(value)
            start += count
        part = three_passes(jnp.concatenate(values, axis=0), high_ref[...], low_ref[...])

        @pl.when(pl.program_id(0) == 0)
        def _():
            out_ref[...] = jnp.zeros_like(out_ref)

        for slot in range(slots):
            out_ref[shard_ref[slot]] += part[slot * rows : (slot + 1) * rows]

    return pl.pallas_call(
        kernel,
        grid_spec=pltpu.PrefetchScalarGridSpec(
            num_scalar_prefetch=1,
            grid=(coefficients // width,),
            in_specs=[
                pl.BlockSpec((width, samples), lambda p, shard: (p, 0)),
                pl.BlockSpec((width, samples), lambda p, shard: (p, 0)),
                pl.BlockSpec((rows, width), lambda p, shard: (chunk, p)),
            ]
            + [pl.BlockSpec((rows, width), lambda p, shard: (0, p)) for _ in pieces],
            out_specs=pl.BlockSpec((slots, rows, samples), lambda p, shard: (0, 0, 0)),
        ),
        out_shape=jax.ShapeDtypeStruct((slots, rows, samples), jnp.float32),
        compiler_params=pltpu.CompilerParams(vmem_limit_bytes=24 << 20),
        name="project",
    )(shards, tall_high, tall_low, own, *pieces)


def multiply(high, low, taps, blocks, places, shards):
    samples, coefficients = high.shape
    _, components, epochs, _ = taps.shape
    slots, rows, _ = blocks[0].shape
    width = math.gcd(coefficients, 5120)
    count = len(blocks)

    def kernel(shard_ref, place_ref, high_ref, low_ref, taps_ref, *refs):
        block_refs = refs[:count]
        out_refs = refs[count:-1]
        weighted_ref = refs[-1]

        @pl.when(pl.program_id(0) == 0)
        def _():
            sums = [0.0] * components
            for source in range(count):
                block = block_refs[source][...].reshape(slots * rows, samples)
                for c in range(components):
                    piece = block[:, c * epochs : (c + 1) * epochs]
                    factor = taps_ref[place_ref[source], c]
                    sums[c] = sums[c] + lax.dot_general(
                        piece, factor, ALONG, precision=HIGHEST, preferred_element_type=jnp.float32
                    )
            weighted_ref[...] = jnp.concatenate(sums, axis=1).reshape(slots, rows, samples)

        weighted = jnp.concatenate([weighted_ref[shard_ref[slot]] for slot in range(slots)], axis=0)
        product = three_passes(weighted, high_ref[...], low_ref[...])
        for slot in range(slots):
            out_refs[slot][...] = product[slot * rows : (slot + 1) * rows]

    return pl.pallas_call(
        kernel,
        grid_spec=pltpu.PrefetchScalarGridSpec(
            num_scalar_prefetch=2,
            grid=(coefficients // width,),
            in_specs=[
                pl.BlockSpec((samples, width), lambda p, shard, place: (0, p)),
                pl.BlockSpec((samples, width), lambda p, shard, place: (0, p)),
                pl.BlockSpec(taps.shape, lambda p, shard, place: (0, 0, 0, 0)),
            ]
            + [pl.BlockSpec((slots, rows, samples), lambda p, shard, place: (0, 0, 0)) for _ in blocks],
            out_specs=[pl.BlockSpec((rows, width), lambda p, shard, place: (0, p)) for _ in range(slots)],
            scratch_shapes=[pltpu.VMEM((slots, rows, samples), jnp.float32)],
        ),
        out_shape=[jax.ShapeDtypeStruct((rows, coefficients), jnp.float32) for _ in range(slots)],
        compiler_params=pltpu.CompilerParams(vmem_limit_bytes=24 << 20),
        name="multiply",
    )(shards, places, high, low, taps, *blocks)


def step_pairs(length, step, parity):
    pairs = []
    for low in range(parity, length - 1, 2):
        if low - step + 1 >= 0:
            pairs.append((low, low + 1))
        if low + step < length:
            pairs.append((low + 1, low))
    return pairs


def gather_along(value, length):
    arrived = {(0, 0): value, (1, 0): value}
    for step in range(1, length):
        for parity in (0, 1):
            pairs = step_pairs(length, step, parity)
            source = arrived.get((1 - parity, step - 1))
            if pairs:
                arrived[parity, step] = lax.ppermute(source, "tm", pairs)
    return [
        [arrived[key] for key in ((0, slot), (1, length - slot)) if key in arrived] for slot in range(1, length)
    ]


def reduce_along(slots, length):
    pending = {}
    for step in range(length - 1, 0, -1):
        for parity in (0, 1):
            pairs = step_pairs(length, step, parity)
            if pairs:
                value = slots[step] if parity == 0 else slots[length - step]
                if (1 - parity, step + 1) in pending:
                    value = value + pending[1 - parity, step + 1]
                pending[parity, step] = lax.ppermute(value, "tm", [(b, a) for a, b in pairs])
    result = slots[0]
    for parity in (0, 1):
        if (parity, 1) in pending:
            result = result + pending[parity, 1]
    return result


def exchange(value, length):
    if length <= 8 and length & (length - 1) == 0:
        others = [lax.ppermute(value, "tm", [(i, i ^ by) for i in range(length)]) for by in range(1, length)]
        return [value] + others, lax.axis_index("tm") ^ jnp.arange(length, dtype=jnp.int32)
    gathered = lax.all_gather(value, "tm", axis=0)
    return [gathered[i] for i in range(length)], jnp.arange(length, dtype=jnp.int32)


def body(design, filter_taps, probes):
    components, epochs, coefficients = design.shape
    length = lax.axis_size("tm")
    place = lax.axis_index("tm")
    own = probes.T
    columns = own.shape[0]
    chunks = 2 if columns % 16 == 0 else 1
    rows = columns // chunks
    direction = 1 - 2 * (place % 2)
    shards = (place + direction * jnp.arange(length, dtype=jnp.int32)) % length
    taps = normal_rows(filter_taps, place, epochs, length * epochs)
    high, low, tall_high, tall_low = split_design(design)
    results = []
    for chunk in range(chunks):
        arrivals = gather_along(own[chunk * rows : (chunk + 1) * rows], length)
        partial = project(tall_high, tall_low, own, chunk, arrivals, shards)
        projected = jnp.sum(lax.all_gather(partial, "param", axis=0), axis=0)
        blocks, places = exchange(projected, length)
        slots = multiply(high, low, taps, blocks, places, shards)
        results.append(reduce_along(slots, length))
    return jnp.concatenate(results, axis=0).T


def solution(mesh):
    in_specs = (P(None, ("groups", "tm"), "param"), P(), P("param", ("groups", "tm")))
    out_specs = P("param", ("groups", "tm"))
    return jax.shard_map(body, mesh=mesh, in_specs=in_specs, out_specs=out_specs, check_vma=False)
```

```python
import math

import jax
import jax.numpy as jnp
from jax import lax
from jax.experimental import pallas as pl
from jax.experimental.pallas import tpu as pltpu
from jax.sharding import PartitionSpec as P

SHORT = pl.CostEstimate(flops=1, bytes_accessed=1, transcendentals=0)
HIGHEST = lax.Precision.HIGHEST
ALONG = (((1,), (1,)), ((), ()))
ACROSS = (((1,), (0,)), ((), ()))


def split(value):
    high = value.astype(jnp.bfloat16)
    return high, (value - high.astype(jnp.float32)).astype(jnp.bfloat16)


def three_passes(left, right_high, right_low):
    left_high, left_low = split(left)
    height = left.shape[0]
    both = jnp.concatenate([left_high, left_low], axis=0)
    first = lax.dot_general(both, right_high, ACROSS, preferred_element_type=jnp.float32)
    last = lax.dot_general(left_high, right_low, ACROSS, preferred_element_type=jnp.float32)
    return first[:height] + (first[height:] + last)


def split_design(design):
    components, epochs, coefficients = design.shape
    samples = components * epochs
    width = math.gcd(coefficients, 2048)

    def kernel(design_ref, high_ref, low_ref, tall_high_ref, tall_low_ref):
        block = design_ref[...].reshape(samples, width)
        high_ref[...], low_ref[...] = split(block)
        tall_high_ref[...], tall_low_ref[...] = split(block.T)

    flat = jax.ShapeDtypeStruct((samples, coefficients), jnp.bfloat16)
    tall = jax.ShapeDtypeStruct((coefficients, samples), jnp.bfloat16)
    return pl.pallas_call(
        kernel,
        grid=(coefficients // width,),
        in_specs=[pl.BlockSpec((components, epochs, width), lambda p: (0, 0, p))],
        out_specs=[pl.BlockSpec((samples, width), lambda p: (0, p))] * 2
        + [pl.BlockSpec((width, samples), lambda p: (p, 0))] * 2,
        out_shape=[flat, flat, tall, tall],
        compiler_params=pltpu.CompilerParams(vmem_limit_bytes=16 << 20),
        cost_estimate=SHORT,
        name="split_design",
    )(design)


def normal_rows(filter_taps, block_index, epochs, total):
    components, tap_count = filter_taps.shape
    lanes = -(-(total + tap_count) // 128) * 128
    pad = jnp.zeros((components, lanes - tap_count), jnp.float32)
    ascending = jnp.concatenate([filter_taps, pad], axis=1)[:, None, :]
    descending = jnp.concatenate([filter_taps[:, ::-1], pad], axis=1)[:, None, :]

    def kernel(index_ref, ascending_ref, descending_ref, out_ref, forward_ref):
        rising = jnp.broadcast_to(ascending_ref[0], (epochs, lanes))
        falling = jnp.broadcast_to(descending_ref[0], (epochs, lanes))
        for block in range(total // epochs):
            shift = (block * epochs - (tap_count - 1)) % lanes
            rolled = pltpu.roll(falling, shift, 1, stride=1, stride_axis=0)
            forward_ref[block * epochs : (block + 1) * epochs, :] = rolled[:, :total]
        staggered = pltpu.roll(rising, 0, 1, stride=1, stride_axis=0)
        backward = pltpu.roll(staggered, index_ref[0] * epochs, 1)[:, :total]
        rows = jnp.dot(backward, forward_ref[...], precision=HIGHEST, preferred_element_type=jnp.float32)
        for block in range(total // epochs):
            out_ref[block, 0] = rows[:, block * epochs : (block + 1) * epochs]

    return pl.pallas_call(
        kernel,
        grid_spec=pltpu.PrefetchScalarGridSpec(
            num_scalar_prefetch=1,
            grid=(components,),
            in_specs=[
                pl.BlockSpec((1, 1, lanes), lambda c, index: (c, 0, 0)),
                pl.BlockSpec((1, 1, lanes), lambda c, index: (c, 0, 0)),
            ],
            out_specs=pl.BlockSpec((total // epochs, 1, epochs, epochs), lambda c, index: (0, c, 0, 0)),
            scratch_shapes=[pltpu.VMEM((total, total), jnp.float32)],
        ),
        out_shape=jax.ShapeDtypeStruct((total // epochs, components, epochs, epochs), jnp.float32),
        compiler_params=pltpu.CompilerParams(vmem_limit_bytes=(4 << 20) + 4 * total * total),
        cost_estimate=SHORT,
        name="normal_rows",
    )(jnp.reshape(block_index, (1,)).astype(jnp.int32), ascending, descending)


def project(tall_high, tall_low, own, chunk, arrivals, shards):
    coefficients, samples = tall_high.shape
    slots = len(arrivals) + 1
    rows = arrivals[0][0].shape[0]
    width = math.gcd(coefficients, 5120)
    counts = [len(pieces) for pieces in arrivals]
    pieces = [piece for group in arrivals for piece in group]

    def kernel(shard_ref, high_ref, low_ref, own_ref, *refs):
        *piece_refs, out_ref = refs
        values = [own_ref[...]]
        start = 0
        for count in counts:
            value = piece_refs[start][...]
            for ref in piece_refs[start + 1 : start + count]:
                value = value + ref[...]
            values.append(value)
            start += count
        part = three_passes(jnp.concatenate(values, axis=0), high_ref[...], low_ref[...])

        @pl.when(pl.program_id(0) == 0)
        def _():
            out_ref[...] = jnp.zeros_like(out_ref)

        for slot in range(slots):
            out_ref[shard_ref[slot]] += part[slot * rows : (slot + 1) * rows]

    return pl.pallas_call(
        kernel,
        grid_spec=pltpu.PrefetchScalarGridSpec(
            num_scalar_prefetch=1,
            grid=(coefficients // width,),
            in_specs=[
                pl.BlockSpec((width, samples), lambda p, shard: (p, 0)),
                pl.BlockSpec((width, samples), lambda p, shard: (p, 0)),
                pl.BlockSpec((rows, width), lambda p, shard: (chunk, p)),
            ]
            + [pl.BlockSpec((rows, width), lambda p, shard: (0, p)) for _ in pieces],
            out_specs=pl.BlockSpec((slots, rows, samples), lambda p, shard: (0, 0, 0)),
        ),
        out_shape=jax.ShapeDtypeStruct((slots, rows, samples), jnp.float32),
        compiler_params=pltpu.CompilerParams(vmem_limit_bytes=24 << 20),
        cost_estimate=SHORT,
        name="project",
    )(shards, tall_high, tall_low, own, *pieces)


def multiply(high, low, taps, blocks, places, shards):
    samples, coefficients = high.shape
    _, components, epochs, _ = taps.shape
    slots, rows, _ = blocks[0].shape
    width = math.gcd(coefficients, 5120)
    count = len(blocks)

    def kernel(shard_ref, place_ref, high_ref, low_ref, taps_ref, *refs):
        block_refs = refs[:count]
        out_refs = refs[count:-1]
        weighted_ref = refs[-1]

        @pl.when(pl.program_id(0) == 0)
        def _():
            sums = [0.0] * components
            for source in range(count):
                block = block_refs[source][...].reshape(slots * rows, samples)
                for c in range(components):
                    piece = block[:, c * epochs : (c + 1) * epochs]
                    factor = taps_ref[place_ref[source], c]
                    sums[c] = sums[c] + lax.dot_general(
                        piece, factor, ALONG, precision=HIGHEST, preferred_element_type=jnp.float32
                    )
            weighted_ref[...] = jnp.concatenate(sums, axis=1).reshape(slots, rows, samples)

        weighted = jnp.concatenate([weighted_ref[shard_ref[slot]] for slot in range(slots)], axis=0)
        product = three_passes(weighted, high_ref[...], low_ref[...])
        for slot in range(slots):
            out_refs[slot][...] = product[slot * rows : (slot + 1) * rows]

    return pl.pallas_call(
        kernel,
        grid_spec=pltpu.PrefetchScalarGridSpec(
            num_scalar_prefetch=2,
            grid=(coefficients // width,),
            in_specs=[
                pl.BlockSpec((samples, width), lambda p, shard, place: (0, p)),
                pl.BlockSpec((samples, width), lambda p, shard, place: (0, p)),
                pl.BlockSpec(taps.shape, lambda p, shard, place: (0, 0, 0, 0)),
            ]
            + [pl.BlockSpec((slots, rows, samples), lambda p, shard, place: (0, 0, 0)) for _ in blocks],
            out_specs=[pl.BlockSpec((rows, width), lambda p, shard, place: (0, p)) for _ in range(slots)],
            scratch_shapes=[pltpu.VMEM((slots, rows, samples), jnp.float32)],
        ),
        out_shape=[jax.ShapeDtypeStruct((rows, coefficients), jnp.float32) for _ in range(slots)],
        compiler_params=pltpu.CompilerParams(vmem_limit_bytes=24 << 20),
        cost_estimate=SHORT,
        name="multiply",
    )(shards, places, high, low, taps, *blocks)


def add_up(shares):
    count, slots, rows, samples = shares.shape

    def kernel(shares_ref, out_ref):
        value = shares_ref[0]
        for share in range(1, count):
            value = value + shares_ref[share]
        out_ref[...] = value

    return pl.pallas_call(
        kernel,
        out_shape=jax.ShapeDtypeStruct((slots, rows, samples), jnp.float32),
        compiler_params=pltpu.CompilerParams(vmem_limit_bytes=8 << 20),
        cost_estimate=SHORT,
        name="add_up",
    )(shares)


def step_pairs(length, step, parity):
    pairs = []
    for low in range(parity, length - 1, 2):
        if low - step + 1 >= 0:
            pairs.append((low, low + 1))
        if low + step < length:
            pairs.append((low + 1, low))
    return pairs


def after(value, *others):
    return lax.optimization_barrier((value,) + others)[0]


class Gather:
    def __init__(self, value, length):
        self.length = length
        self.arrived = {(0, 0): value, (1, 0): value}
        self.done = 0
        self.latest = [value]

    def step(self, count=1):
        for _ in range(count):
            if self.done == self.length - 1:
                return
            self.done += 1
            self.latest = []
            for parity in (0, 1):
                pairs = step_pairs(self.length, self.done, parity)
                if pairs:
                    value = lax.ppermute(self.arrived[1 - parity, self.done - 1], "tm", pairs)
                    self.arrived[parity, self.done] = value
                    self.latest.append(value)

    def slots(self):
        self.step(self.length)
        return [
            [self.arrived[key] for key in ((0, slot), (1, self.length - slot)) if key in self.arrived]
            for slot in range(1, self.length)
        ]


class Reduction:
    def __init__(self, slots, length):
        self.length = length
        self.slots = slots
        self.pending = {}
        self.left = length - 1
        self.latest = []

    def step(self, count=1):
        for _ in range(count):
            if self.left == 0:
                return
            self.latest = []
            for parity in (0, 1):
                pairs = step_pairs(self.length, self.left, parity)
                if pairs:
                    value = self.slots[self.left] if parity == 0 else self.slots[self.length - self.left]
                    if (1 - parity, self.left + 1) in self.pending:
                        value = value + self.pending[1 - parity, self.left + 1]
                    value = lax.ppermute(value, "tm", [(b, a) for a, b in pairs])
                    self.pending[parity, self.left] = value
                    self.latest.append(value)
            self.left -= 1

    def result(self):
        self.step(self.length)
        value = self.slots[0]
        for parity in (0, 1):
            if (parity, 1) in self.pending:
                value = value + self.pending[parity, 1]
        return value


def is_direct(length):
    return length <= 8 and length & (length - 1) == 0


def places_of(length):
    numbers = jnp.arange(length, dtype=jnp.int32)
    return lax.axis_index("tm") ^ numbers if is_direct(length) else numbers


def exchange(value, length):
    if is_direct(length):
        return [value] + [lax.ppermute(value, "tm", [(i, i ^ by) for i in range(length)]) for by in range(1, length)]
    gathered = lax.all_gather(value, "tm", axis=0)
    return [gathered[i] for i in range(length)]


def body(design, filter_taps, probes):
    components, epochs, coefficients = design.shape
    length = lax.axis_size("tm")
    place = lax.axis_index("tm")
    own = probes.T
    columns = own.shape[0]
    chunks = 2 if columns % 16 == 0 else 1
    rows = columns // chunks
    direction = 1 - 2 * (place % 2)
    shards = (place + direction * jnp.arange(length, dtype=jnp.int32)) % length
    taps = normal_rows(filter_taps, place, epochs, length * epochs)
    places = places_of(length)
    high, low, tall_high, tall_low = split_design(after(design, taps, shards, places))
    parts = []
    for chunk in range(chunks):
        value = own[chunk * rows : (chunk + 1) * rows]
        if parts:
            value = after(value, *last_source)
        gather = Gather(value, length)
        if chunk == 0:
            gather.step(length - 2)
            last_source = gather.latest
            gather.step()
        parts.append(gather)
    results = []
    for chunk, gather in enumerate(parts):
        behind = parts[chunk + 1] if chunk + 1 < chunks else (results[-1] if results else None)
        if behind is not None:
            behind.step()
        partial = project(tall_high, tall_low, own, chunk, gather.slots(), shards)
        if behind is not None:
            partial = after(partial, *behind.latest)
            behind.step()
        projected = add_up(lax.all_gather(partial, "param", axis=0))
        blocks = exchange(projected, length)
        if behind is not None:
            blocks[-1] = after(blocks[-1], *behind.latest)
            behind.step()
        results.append(Reduction(multiply(high, low, taps, blocks, places, shards), length))
    return jnp.concatenate([reduction.result() for reduction in results], axis=0).T


def solution(mesh):
    in_specs = (P(None, ("groups", "tm"), "param"), P(), P("param", ("groups", "tm")))
    out_specs = P("param", ("groups", "tm"))
    return jax.shard_map(body, mesh=mesh, in_specs=in_specs, out_specs=out_specs, check_vma=False)
```

```python
import math

import jax
import jax.numpy as jnp
from jax import lax
from jax.experimental import pallas as pl
from jax.experimental.pallas import tpu as pltpu
from jax.sharding import PartitionSpec as P


def cost(size):
    return pl.CostEstimate(flops=1, bytes_accessed=size, transcendentals=0)


SHORT = cost(1)
LONG = cost(12_000_000)
HIGHEST = lax.Precision.HIGHEST
ALONG = (((1,), (1,)), ((), ()))
ACROSS = (((1,), (0,)), ((), ()))


def split(value):
    high = value.astype(jnp.bfloat16)
    return high, (value - high.astype(jnp.float32)).astype(jnp.bfloat16)


def three_passes(left, right_high, right_low):
    left_high, left_low = split(left)
    height = left.shape[0]
    both = jnp.concatenate([left_high, left_low], axis=0)
    first = lax.dot_general(both, right_high, ACROSS, preferred_element_type=jnp.float32)
    last = lax.dot_general(left_high, right_low, ACROSS, preferred_element_type=jnp.float32)
    return first[:height] + (first[height:] + last)


def split_design(design):
    components, epochs, coefficients = design.shape
    samples = components * epochs
    width = math.gcd(coefficients, 2048)

    def kernel(design_ref, high_ref, low_ref, tall_high_ref, tall_low_ref):
        block = design_ref[...].reshape(samples, width)
        high_ref[...], low_ref[...] = split(block)
        tall_high_ref[...], tall_low_ref[...] = split(block.T)

    flat = jax.ShapeDtypeStruct((samples, coefficients), jnp.bfloat16)
    tall = jax.ShapeDtypeStruct((coefficients, samples), jnp.bfloat16)
    return pl.pallas_call(
        kernel,
        grid=(coefficients // width,),
        in_specs=[pl.BlockSpec((components, epochs, width), lambda p: (0, 0, p))],
        out_specs=[pl.BlockSpec((samples, width), lambda p: (0, p))] * 2
        + [pl.BlockSpec((width, samples), lambda p: (p, 0))] * 2,
        out_shape=[flat, flat, tall, tall],
        compiler_params=pltpu.CompilerParams(vmem_limit_bytes=16 << 20),
        cost_estimate=SHORT,
        name="split_design",
    )(design)


def normal_rows(filter_taps, block_index, epochs, total):
    components, tap_count = filter_taps.shape
    lanes = -(-(total + tap_count) // 128) * 128

    def kernel(index_ref, taps_ref, out_ref, lag_ref):
        for c in range(components):
            row = jnp.concatenate([taps_ref[c : c + 1], jnp.zeros((1, lanes - tap_count), jnp.float32)], axis=1)
            square = jnp.broadcast_to(row, (epochs, lanes))
            for block in range(total // epochs):
                rolled = pltpu.roll(square, block * epochs, 1, stride=1, stride_axis=0)
                lag_ref[block * epochs : (block + 1) * epochs, :] = rolled[:, :total]
            staggered = pltpu.roll(square, 0, 1, stride=1, stride_axis=0)
            weight = pltpu.roll(staggered, index_ref[0] * epochs, 1)[:, :total]
            rows = lax.dot_general(weight, lag_ref[...], ALONG, precision=HIGHEST, preferred_element_type=jnp.float32)
            for block in range(total // epochs):
                out_ref[block, c] = rows[:, block * epochs : (block + 1) * epochs]

    return pl.pallas_call(
        kernel,
        grid_spec=pltpu.PrefetchScalarGridSpec(
            num_scalar_prefetch=1,
            grid=(1,),
            in_specs=[pl.BlockSpec((components, tap_count), lambda c, index: (0, 0))],
            out_specs=pl.BlockSpec((total // epochs, components, epochs, epochs), lambda c, index: (0, 0, 0, 0)),
            scratch_shapes=[pltpu.VMEM((total, total), jnp.float32)],
        ),
        out_shape=jax.ShapeDtypeStruct((total // epochs, components, epochs, epochs), jnp.float32),
        compiler_params=pltpu.CompilerParams(vmem_limit_bytes=(8 << 20) + 6 * total * total),
        cost_estimate=SHORT,
        name="normal_rows",
    )(jnp.reshape(block_index, (1,)).astype(jnp.int32), filter_taps)


def project(tall_high, tall_low, own, chunk, arrivals, shards):
    coefficients, samples = tall_high.shape
    slots = len(arrivals) + 1
    rows = arrivals[0][0].shape[0]
    width = math.gcd(coefficients, 5120)
    counts = [len(pieces) for pieces in arrivals]
    pieces = [piece for group in arrivals for piece in group]

    def kernel(shard_ref, high_ref, low_ref, own_ref, *refs):
        *piece_refs, out_ref = refs
        values = [own_ref[...]]
        start = 0
        for count in counts:
            value = piece_refs[start][...]
            for ref in piece_refs[start + 1 : start + count]:
                value = value + ref[...]
            values.append(value)
            start += count
        part = three_passes(jnp.concatenate(values, axis=0), high_ref[...], low_ref[...])

        @pl.when(pl.program_id(0) == 0)
        def _():
            out_ref[...] = jnp.zeros_like(out_ref)

        for slot in range(slots):
            out_ref[shard_ref[slot]] += part[slot * rows : (slot + 1) * rows]

    return pl.pallas_call(
        kernel,
        grid_spec=pltpu.PrefetchScalarGridSpec(
            num_scalar_prefetch=1,
            grid=(coefficients // width,),
            in_specs=[
                pl.BlockSpec((width, samples), lambda p, shard: (p, 0)),
                pl.BlockSpec((width, samples), lambda p, shard: (p, 0)),
                pl.BlockSpec((rows, width), lambda p, shard: (chunk, p)),
            ]
            + [pl.BlockSpec((rows, width), lambda p, shard: (0, p)) for _ in pieces],
            out_specs=pl.BlockSpec((slots, rows, samples), lambda p, shard: (0, 0, 0)),
        ),
        out_shape=jax.ShapeDtypeStruct((slots, rows, samples), jnp.float32),
        compiler_params=pltpu.CompilerParams(vmem_limit_bytes=24 << 20),
        cost_estimate=LONG,
        name="project",
    )(shards, tall_high, tall_low, own, *pieces)


def multiply(high, low, taps, blocks, places, shards):
    samples, coefficients = high.shape
    _, components, epochs, _ = taps.shape
    slots, rows, _ = blocks[0].shape
    width = math.gcd(coefficients, 5120)
    count = len(blocks)

    def kernel(shard_ref, place_ref, high_ref, low_ref, taps_ref, *refs):
        block_refs = refs[:count]
        out_refs = refs[count:-1]
        weighted_ref = refs[-1]

        @pl.when(pl.program_id(0) == 0)
        def _():
            sums = [0.0] * components
            for source in range(count):
                block = block_refs[source][...].reshape(slots * rows, samples)
                for c in range(components):
                    piece = block[:, c * epochs : (c + 1) * epochs]
                    factor = taps_ref[place_ref[source], c]
                    sums[c] = sums[c] + lax.dot_general(
                        piece, factor, ALONG, precision=HIGHEST, preferred_element_type=jnp.float32
                    )
            weighted_ref[...] = jnp.concatenate(sums, axis=1).reshape(slots, rows, samples)

        weighted = jnp.concatenate([weighted_ref[shard_ref[slot]] for slot in range(slots)], axis=0)
        product = three_passes(weighted, high_ref[...], low_ref[...])
        for slot in range(slots):
            out_refs[slot][...] = product[slot * rows : (slot + 1) * rows]

    return pl.pallas_call(
        kernel,
        grid_spec=pltpu.PrefetchScalarGridSpec(
            num_scalar_prefetch=2,
            grid=(coefficients // width,),
            in_specs=[
                pl.BlockSpec((samples, width), lambda p, shard, place: (0, p)),
                pl.BlockSpec((samples, width), lambda p, shard, place: (0, p)),
                pl.BlockSpec(taps.shape, lambda p, shard, place: (0, 0, 0, 0)),
            ]
            + [pl.BlockSpec((slots, rows, samples), lambda p, shard, place: (0, 0, 0)) for _ in blocks],
            out_specs=[pl.BlockSpec((rows, width), lambda p, shard, place: (0, p)) for _ in range(slots)],
            scratch_shapes=[pltpu.VMEM((slots, rows, samples), jnp.float32)],
        ),
        out_shape=[jax.ShapeDtypeStruct((rows, coefficients), jnp.float32) for _ in range(slots)],
        compiler_params=pltpu.CompilerParams(vmem_limit_bytes=24 << 20),
        cost_estimate=SHORT,
        name="multiply",
    )(shards, places, high, low, taps, *blocks)


def add_up(shares):
    count, slots, rows, samples = shares.shape

    def kernel(shares_ref, out_ref):
        value = shares_ref[0]
        for share in range(1, count):
            value = value + shares_ref[share]
        out_ref[...] = value

    return pl.pallas_call(
        kernel,
        out_shape=jax.ShapeDtypeStruct((slots, rows, samples), jnp.float32),
        compiler_params=pltpu.CompilerParams(vmem_limit_bytes=8 << 20),
        cost_estimate=SHORT,
        name="add_up",
    )(shares)


def total_of(values):
    rows, coefficients = values[0].shape
    width = math.gcd(coefficients, 5120)

    def kernel(*refs):
        value = refs[0][...]
        for ref in refs[1:-1]:
            value = value + ref[...]
        refs[-1][...] = value

    return pl.pallas_call(
        kernel,
        grid=(coefficients // width,),
        in_specs=[pl.BlockSpec((rows, width), lambda p: (0, p)) for _ in values],
        out_specs=pl.BlockSpec((rows, width), lambda p: (0, p)),
        out_shape=jax.ShapeDtypeStruct((rows, coefficients), jnp.float32),
        compiler_params=pltpu.CompilerParams(vmem_limit_bytes=8 << 20),
        cost_estimate=LONG,
        name="total_of",
    )(*values)


def step_pairs(length, step, parity):
    pairs = []
    for low in range(parity, length - 1, 2):
        if low - step + 1 >= 0:
            pairs.append((low, low + 1))
        if low + step < length:
            pairs.append((low + 1, low))
    return pairs


def after(value, *others):
    return lax.optimization_barrier((value,) + others)[0]


class Gather:
    def __init__(self, value, length):
        self.length = length
        self.arrived = {(0, 0): value, (1, 0): value}
        self.done = 0
        self.latest = [value]

    def step(self, count=1, behind=()):
        for _ in range(min(count, self.length - 1 - self.done)):
            self.done += 1
            self.latest = []
            for parity in (0, 1):
                pairs = step_pairs(self.length, self.done, parity)
                if pairs:
                    value = self.arrived[1 - parity, self.done - 1]
                    if behind:
                        value = after(value, *behind)
                    value = lax.ppermute(value, "tm", pairs)
                    self.arrived[parity, self.done] = value
                    self.latest.append(value)

    def slots(self, behind=()):
        self.step(self.length)
        slots = [
            [self.arrived[key] for key in ((0, slot), (1, self.length - slot)) if key in self.arrived]
            for slot in range(1, self.length)
        ]
        if behind:
            slots[-1][-1] = after(slots[-1][-1], *behind)
        return slots


class Reduction:
    def __init__(self, slots, length):
        self.length = length
        self.slots = slots
        self.pending = {}
        self.left = length - 1
        self.latest = []

    def step(self, count=1, behind=()):
        for _ in range(min(count, self.left)):
            self.latest = []
            for parity in (0, 1):
                pairs = step_pairs(self.length, self.left, parity)
                if pairs:
                    value = self.slots[self.left] if parity == 0 else self.slots[self.length - self.left]
                    if (1 - parity, self.left + 1) in self.pending:
                        waiting = self.pending[1 - parity, self.left + 1]
                        if behind:
                            waiting = after(waiting, *behind)
                        value = value + waiting
                    value = lax.ppermute(value, "tm", [(b, a) for a, b in pairs])
                    self.pending[parity, self.left] = value
                    self.latest.append(value)
            self.left -= 1

    def result(self):
        self.step(self.length)
        return total_of([self.slots[0]] + [self.pending[key] for key in ((0, 1), (1, 1)) if key in self.pending])


def is_direct(length):
    return length <= 8 and length & (length - 1) == 0


def places_of(length):
    numbers = jnp.arange(length, dtype=jnp.int32)
    return lax.axis_index("tm") ^ numbers if is_direct(length) else numbers


def exchange(value, length):
    if is_direct(length):
        return [value] + [lax.ppermute(value, "tm", [(i, i ^ by) for i in range(length)]) for by in range(1, length)]
    gathered = lax.all_gather(value, "tm", axis=0)
    return [gathered[i] for i in range(length)]


def body(design, filter_taps, probes):
    components, epochs, coefficients = design.shape
    length = lax.axis_size("tm")
    place = lax.axis_index("tm")
    own = probes.T
    columns = own.shape[0]
    chunks = 2 if columns % 16 == 0 else 1
    rows = columns // chunks
    direction = 1 - 2 * (place % 2)
    shards = (place + direction * jnp.arange(length, dtype=jnp.int32)) % length
    places = places_of(length)
    taps = normal_rows(filter_taps, place, epochs, length * epochs)
    high, low, tall_high, tall_low = split_design(after(design, taps, shards, places))

    def summed(partial):
        return add_up(lax.all_gather(partial, "param", axis=0))

    def multiplied(blocks):
        return Reduction(multiply(high, low, taps, blocks, places, shards), length)

    first = Gather(own[:rows], length)
    first.step()
    first.step(behind=[high])
    waited = first.latest
    first.step(length)
    if chunks == 1:
        partial = project(tall_high, tall_low, own, 0, first.slots(), shards)
        return multiplied(exchange(summed(partial), length)).result().T
    second = Gather(after(own[rows:], *waited), length)
    second.step()
    partial = project(tall_high, tall_low, own, 0, first.slots(), shards)
    projected = summed(partial)
    second.step(behind=[projected])
    ahead = multiplied(exchange(projected, length))
    ahead.step()
    second.step(length, behind=[ahead.slots[0]])
    partial = project(tall_high, tall_low, own, 1, second.slots(behind=ahead.latest[:1]), shards)
    ahead.step()
    projected = summed(partial)
    ahead.step(length, behind=[projected])
    start = ahead.result()
    trailing = multiplied(exchange(projected, length))
    trailing.step()
    trailing.step(behind=[start])
    return jnp.concatenate([start, trailing.result()], axis=0).T


def solution(mesh):
    in_specs = (P(None, ("groups", "tm"), "param"), P(), P("param", ("groups", "tm")))
    out_specs = P("param", ("groups", "tm"))
    return jax.shard_map(body, mesh=mesh, in_specs=in_specs, out_specs=out_specs, check_vma=False)
```

```python
import math

import jax
import jax.numpy as jnp
from jax import lax
from jax.experimental import pallas as pl
from jax.experimental.pallas import tpu as pltpu
from jax.sharding import PartitionSpec as P


def cost(size):
    return pl.CostEstimate(flops=1, bytes_accessed=size, transcendentals=0)


SHORT = cost(1)
LONG = cost(200_000_000)
HIGHEST = lax.Precision.HIGHEST
ALONG = (((1,), (1,)), ((), ()))
ACROSS = (((1,), (0,)), ((), ()))


def split(value):
    high = value.astype(jnp.bfloat16)
    return high, (value - high.astype(jnp.float32)).astype(jnp.bfloat16)


def three_passes(left, right_high, right_low):
    left_high, left_low = split(left)
    height = left.shape[0]
    both = jnp.concatenate([left_high, left_low], axis=0)
    first = lax.dot_general(both, right_high, ACROSS, preferred_element_type=jnp.float32)
    last = lax.dot_general(left_high, right_low, ACROSS, preferred_element_type=jnp.float32)
    return first[:height] + (first[height:] + last)


def split_design(design, earlier):
    components, epochs, coefficients = design.shape
    samples = components * epochs
    width = math.gcd(coefficients, 2048)

    def kernel(design_ref, *refs):
        high_ref, low_ref, tall_high_ref, tall_low_ref = refs[-4:]
        block = design_ref[...].reshape(samples, width)
        high_ref[...], low_ref[...] = split(block)
        tall_high_ref[...], tall_low_ref[...] = split(block.T)

    flat = jax.ShapeDtypeStruct((samples, coefficients), jnp.bfloat16)
    tall = jax.ShapeDtypeStruct((coefficients, samples), jnp.bfloat16)
    return pl.pallas_call(
        kernel,
        grid=(coefficients // width,),
        in_specs=[pl.BlockSpec((components, epochs, width), lambda p: (0, 0, p))]
        + [pl.BlockSpec(memory_space=pl.ANY)] * len(earlier),
        out_specs=[pl.BlockSpec((samples, width), lambda p: (0, p))] * 2
        + [pl.BlockSpec((width, samples), lambda p: (p, 0))] * 2,
        out_shape=[flat, flat, tall, tall],
        compiler_params=pltpu.CompilerParams(vmem_limit_bytes=16 << 20),
        cost_estimate=SHORT,
        name="split_design",
    )(design, *earlier)


def normal_rows(filter_taps, block_index, epochs, total):
    components, tap_count = filter_taps.shape
    lanes = -(-(total + tap_count) // 128) * 128

    def kernel(index_ref, taps_ref, out_ref, lag_ref):
        for c in range(components):
            row = jnp.concatenate([taps_ref[c : c + 1], jnp.zeros((1, lanes - tap_count), jnp.float32)], axis=1)
            square = jnp.broadcast_to(row, (epochs, lanes))
            for block in range(total // epochs):
                rolled = pltpu.roll(square, block * epochs, 1, stride=1, stride_axis=0)
                lag_ref[block * epochs : (block + 1) * epochs, :] = rolled[:, :total]
            staggered = pltpu.roll(square, 0, 1, stride=1, stride_axis=0)
            weight = pltpu.roll(staggered, index_ref[0] * epochs, 1)[:, :total]
            rows = lax.dot_general(weight, lag_ref[...], ALONG, precision=HIGHEST, preferred_element_type=jnp.float32)
            for block in range(total // epochs):
                out_ref[block, c] = rows[:, block * epochs : (block + 1) * epochs]

    return pl.pallas_call(
        kernel,
        grid_spec=pltpu.PrefetchScalarGridSpec(
            num_scalar_prefetch=1,
            grid=(1,),
            in_specs=[pl.BlockSpec((components, tap_count), lambda c, index: (0, 0))],
            out_specs=pl.BlockSpec((total // epochs, components, epochs, epochs), lambda c, index: (0, 0, 0, 0)),
            scratch_shapes=[pltpu.VMEM((total, total), jnp.float32)],
        ),
        out_shape=jax.ShapeDtypeStruct((total // epochs, components, epochs, epochs), jnp.float32),
        compiler_params=pltpu.CompilerParams(vmem_limit_bytes=(8 << 20) + 6 * total * total),
        cost_estimate=SHORT,
        name="normal_rows",
    )(jnp.reshape(block_index, (1,)).astype(jnp.int32), filter_taps)


def project(tall_high, tall_low, own, chunk, arrivals, shards, tile):
    coefficients, samples = tall_high.shape
    slots = len(arrivals) + 1
    rows = arrivals[0][0].shape[0]
    width = math.gcd(coefficients, 5120)
    counts = [len(pieces) for pieces in arrivals]
    pieces = [piece for group in arrivals for piece in group]

    def kernel(shard_ref, high_ref, low_ref, own_ref, *refs):
        *piece_refs, _, out_ref = refs
        values = [own_ref[...]]
        start = 0
        for count in counts:
            value = piece_refs[start][...]
            for ref in piece_refs[start + 1 : start + count]:
                value = value + ref[...]
            values.append(value)
            start += count
        part = three_passes(jnp.concatenate(values, axis=0), high_ref[...], low_ref[...])

        @pl.when(pl.program_id(0) == 0)
        def _():
            out_ref[...] = jnp.zeros_like(out_ref)

        for slot in range(slots):
            out_ref[shard_ref[slot]] += part[slot * rows : (slot + 1) * rows]

    return pl.pallas_call(
        kernel,
        grid_spec=pltpu.PrefetchScalarGridSpec(
            num_scalar_prefetch=1,
            grid=(coefficients // width,),
            in_specs=[
                pl.BlockSpec((width, samples), lambda p, shard: (p, 0)),
                pl.BlockSpec((width, samples), lambda p, shard: (p, 0)),
                pl.BlockSpec((rows, width), lambda p, shard: (chunk, p)),
            ]
            + [pl.BlockSpec((rows, width), lambda p, shard: (0, p)) for _ in pieces]
            + [pl.BlockSpec(memory_space=pl.ANY)],
            out_specs=pl.BlockSpec((slots, rows, samples), lambda p, shard: (0, 0, 0)),
        ),
        out_shape=jax.ShapeDtypeStruct((slots, rows, samples), jnp.float32),
        compiler_params=pltpu.CompilerParams(vmem_limit_bytes=24 << 20),
        cost_estimate=SHORT,
        name="project",
    )(shards, tall_high, tall_low, own, *pieces, tile)


def multiply(high, low, taps, blocks, places, shards, tile):
    samples, coefficients = high.shape
    _, components, epochs, _ = taps.shape
    slots, rows, _ = blocks[0].shape
    width = math.gcd(coefficients, 5120)
    count = len(blocks)

    def kernel(shard_ref, place_ref, high_ref, low_ref, taps_ref, *refs):
        block_refs = refs[:count]
        out_refs = refs[count + 1 : -1]
        weighted_ref = refs[-1]

        @pl.when(pl.program_id(0) == 0)
        def _():
            sums = [0.0] * components
            for source in range(count):
                block = block_refs[source][...].reshape(slots * rows, samples)
                for c in range(components):
                    piece = block[:, c * epochs : (c + 1) * epochs]
                    factor = taps_ref[place_ref[source], c]
                    sums[c] = sums[c] + lax.dot_general(
                        piece, factor, ALONG, precision=HIGHEST, preferred_element_type=jnp.float32
                    )
            weighted_ref[...] = jnp.concatenate(sums, axis=1).reshape(slots, rows, samples)

        weighted = jnp.concatenate([weighted_ref[shard_ref[slot]] for slot in range(slots)], axis=0)
        product = three_passes(weighted, high_ref[...], low_ref[...])
        for slot in range(slots):
            out_refs[slot][...] = product[slot * rows : (slot + 1) * rows]

    return pl.pallas_call(
        kernel,
        grid_spec=pltpu.PrefetchScalarGridSpec(
            num_scalar_prefetch=2,
            grid=(coefficients // width,),
            in_specs=[
                pl.BlockSpec((samples, width), lambda p, shard, place: (0, p)),
                pl.BlockSpec((samples, width), lambda p, shard, place: (0, p)),
                pl.BlockSpec(taps.shape, lambda p, shard, place: (0, 0, 0, 0)),
            ]
            + [pl.BlockSpec((slots, rows, samples), lambda p, shard, place: (0, 0, 0)) for _ in blocks]
            + [pl.BlockSpec(memory_space=pl.ANY)],
            out_specs=[pl.BlockSpec((rows, width), lambda p, shard, place: (0, p)) for _ in range(slots)],
            scratch_shapes=[pltpu.VMEM((slots, rows, samples), jnp.float32)],
        ),
        out_shape=[jax.ShapeDtypeStruct((rows, coefficients), jnp.float32) for _ in range(slots)],
        compiler_params=pltpu.CompilerParams(vmem_limit_bytes=24 << 20),
        cost_estimate=SHORT,
        name="multiply",
    )(shards, places, high, low, taps, *blocks, tile)


def add_up(shares):
    count, slots, rows, samples = shares.shape

    def kernel(shares_ref, out_ref):
        value = shares_ref[0]
        for share in range(1, count):
            value = value + shares_ref[share]
        out_ref[...] = value

    return pl.pallas_call(
        kernel,
        out_shape=jax.ShapeDtypeStruct((slots, rows, samples), jnp.float32),
        compiler_params=pltpu.CompilerParams(vmem_limit_bytes=8 << 20),
        cost_estimate=SHORT,
        name="add_up",
    )(shares)


def total_of(values, tile):
    rows, coefficients = values[0].shape
    width = math.gcd(coefficients, 5120)

    def kernel(*refs):
        value = refs[0][...]
        for ref in refs[1:-2]:
            value = value + ref[...]
        refs[-1][...] = value

    return pl.pallas_call(
        kernel,
        grid=(coefficients // width,),
        in_specs=[pl.BlockSpec((rows, width), lambda p: (0, p)) for _ in values] + [pl.BlockSpec(memory_space=pl.ANY)],
        out_specs=pl.BlockSpec((rows, width), lambda p: (0, p)),
        out_shape=jax.ShapeDtypeStruct((rows, coefficients), jnp.float32),
        compiler_params=pltpu.CompilerParams(vmem_limit_bytes=8 << 20),
        cost_estimate=LONG,
        name="total_of",
    )(*values, tile)


def step_pairs(length, step, parity):
    pairs = []
    for low in range(parity, length - 1, 2):
        if low - step + 1 >= 0:
            pairs.append((low, low + 1))
        if low + step < length:
            pairs.append((low + 1, low))
    return pairs


def mark(tile, *values):
    count = len(values)

    def kernel(tile_ref, *refs):
        refs[count][...] = tile_ref[...]

    return pl.pallas_call(
        kernel,
        in_specs=[pl.BlockSpec(memory_space=pltpu.VMEM)] + [pl.BlockSpec(memory_space=pl.ANY)] * count,
        out_shape=jax.ShapeDtypeStruct(tile.shape, tile.dtype),
        compiler_params=pltpu.CompilerParams(vmem_limit_bytes=1 << 20),
        cost_estimate=LONG,
        name="mark",
    )(tile, *values)


class Gather:
    def __init__(self, value, length):
        self.length = length
        self.arrived = {(0, 0): value, (1, 0): value}
        self.done = 0

    def step(self, count=1):
        for _ in range(min(count, self.length - 1 - self.done)):
            self.done += 1
            for parity in (0, 1):
                pairs = step_pairs(self.length, self.done, parity)
                if pairs:
                    self.arrived[parity, self.done] = lax.ppermute(self.arrived[1 - parity, self.done - 1], "tm", pairs)

    def tie(self, tile, parities=(0, 1)):
        for parity in parities:
            if (parity, self.done) in self.arrived:
                tile, value = lax.optimization_barrier((tile, self.arrived[parity, self.done]))
                self.arrived[parity, self.done] = value
        return tile

    def slots(self):
        self.step(self.length)
        return [
            [self.arrived[key] for key in ((0, slot), (1, self.length - slot)) if key in self.arrived]
            for slot in range(1, self.length)
        ]


class Reduction:
    def __init__(self, slots, length):
        self.length = length
        self.slots = slots
        self.pending = {}
        self.left = length

    def step(self, count=1):
        for _ in range(min(count, self.left - 1)):
            self.left -= 1
            for parity in (0, 1):
                pairs = step_pairs(self.length, self.left, parity)
                if pairs:
                    value = self.slots[self.left] if parity == 0 else self.slots[self.length - self.left]
                    if (1 - parity, self.left + 1) in self.pending:
                        value = value + self.pending[1 - parity, self.left + 1]
                    self.pending[parity, self.left] = lax.ppermute(value, "tm", [(b, a) for a, b in pairs])

    def tie(self, tile, parities=(0, 1)):
        for parity in parities:
            if (parity, self.left) in self.pending:
                tile, value = lax.optimization_barrier((tile, self.pending[parity, self.left]))
                self.pending[parity, self.left] = value
        return tile

    def result(self, tile):
        self.step(self.length)
        waiting = [self.pending[key] for key in ((0, 1), (1, 1)) if key in self.pending]
        return total_of([self.slots[0]] + waiting, tile)


def is_direct(length):
    return length <= 8 and length & (length - 1) == 0


def places_of(length):
    numbers = jnp.arange(length, dtype=jnp.int32)
    return lax.axis_index("tm") ^ numbers if is_direct(length) else numbers


def exchange(value, length):
    if is_direct(length):
        return [value] + [lax.ppermute(value, "tm", [(i, i ^ by) for i in range(length)]) for by in range(1, length)]
    gathered = lax.all_gather(value, "tm", axis=0)
    return [gathered[i] for i in range(length)]


def body(design, filter_taps, probes):
    components, epochs, coefficients = design.shape
    length = lax.axis_size("tm")
    place = lax.axis_index("tm")
    own = probes.T
    columns = own.shape[0]
    chunks = 2 if columns % 16 == 0 else 1
    rows = columns // chunks
    direction = 1 - 2 * (place % 2)
    shards = (place + direction * jnp.arange(length, dtype=jnp.int32)) % length
    places = places_of(length)
    taps = normal_rows(filter_taps, place, epochs, length * epochs)
    tile = jnp.zeros((8, 128), jnp.float32)
    high, low, tall_high, tall_low = split_design(design, [taps, shards, places, tile])

    def summed(partial):
        return add_up(lax.all_gather(partial, "param", axis=0))

    def multiplied(blocks, tile):
        slots = multiply(high, low, taps, blocks, places, shards, tile)
        tile, *slots = lax.optimization_barrier((tile, *slots))
        return Reduction(slots, length), tile

    first = Gather(own[:rows], length)
    first.step()
    tile, taps, shards, places, high, low = lax.optimization_barrier((tile, taps, shards, places, high, low))
    tile = first.tie(tile)
    first.step()
    if chunks == 1:
        partial = project(tall_high, tall_low, own, 0, first.slots(), shards, tile)
        ahead, tile = multiplied(exchange(summed(partial), length), tile)
        return ahead.result(tile).T
    tile = first.tie(tile, (1,))
    first.step(length)
    tile = mark(tile)
    tile, value = lax.optimization_barrier((tile, own[rows:]))
    second = Gather(value, length)
    second.step()
    partial = project(tall_high, tall_low, own, 0, first.slots(), shards, tile)
    projected = summed(partial)
    blocks = exchange(projected, length)
    tile, *blocks = lax.optimization_barrier((tile, *blocks))
    tile = second.tie(tile)
    second.step()
    ahead, tile = multiplied(blocks, mark(tile))
    ahead.step()
    tile = second.tie(tile)
    second.step(length)
    tile = ahead.tie(mark(tile), (0,))
    ahead.step()
    partial = project(tall_high, tall_low, own, 1, second.slots(), shards, mark(tile))
    projected = summed(partial)
    blocks = exchange(projected, length)
    tile = ahead.tie(mark(tile, projected))
    ahead.step(length)
    trailing, tile = multiplied(blocks, mark(tile))
    trailing.step()
    tile = ahead.tie(tile)
    start = ahead.result(tile)
    tile, start = lax.optimization_barrier((tile, start))
    tile = trailing.tie(tile)
    trailing.step()
    return jnp.concatenate([start, trailing.result(tile)], axis=0).T


def solution(mesh):
    in_specs = (P(None, ("groups", "tm"), "param"), P(), P("param", ("groups", "tm")))
    out_specs = P("param", ("groups", "tm"))
    return jax.shard_map(body, mesh=mesh, in_specs=in_specs, out_specs=out_specs, check_vma=False)
```

```python
import math

import jax
import jax.numpy as jnp
from jax import lax
from jax.experimental import pallas as pl
from jax.experimental.pallas import tpu as pltpu
from jax.sharding import PartitionSpec as P


def cost(size):
    return pl.CostEstimate(flops=1, bytes_accessed=size, transcendentals=0)


SHORT = cost(1)
LONG = cost(200_000_000)
HIGHEST = lax.Precision.HIGHEST
ALONG = (((1,), (1,)), ((), ()))
ACROSS = (((1,), (0,)), ((), ()))


def split(value):
    high = value.astype(jnp.bfloat16)
    return high, (value - high.astype(jnp.float32)).astype(jnp.bfloat16)


def three_passes(left, right_high, right_low):
    left_high, left_low = split(left)
    height = left.shape[0]
    both = jnp.concatenate([left_high, left_low], axis=0)
    first = lax.dot_general(both, right_high, ACROSS, preferred_element_type=jnp.float32)
    last = lax.dot_general(left_high, right_low, ACROSS, preferred_element_type=jnp.float32)
    return first[:height] + (first[height:] + last)


def split_design(design, earlier):
    components, epochs, coefficients = design.shape
    samples = components * epochs
    width = math.gcd(coefficients, 2048)

    def kernel(design_ref, *refs):
        high_ref, low_ref, tall_high_ref, tall_low_ref = refs[-4:]
        block = design_ref[...].reshape(samples, width)
        high_ref[...], low_ref[...] = split(block)
        tall_high_ref[...], tall_low_ref[...] = split(block.T)

    flat = jax.ShapeDtypeStruct((samples, coefficients), jnp.bfloat16)
    tall = jax.ShapeDtypeStruct((coefficients, samples), jnp.bfloat16)
    return pl.pallas_call(
        kernel,
        grid=(coefficients // width,),
        in_specs=[pl.BlockSpec((components, epochs, width), lambda p: (0, 0, p))]
        + [pl.BlockSpec(memory_space=pl.ANY)] * len(earlier),
        out_specs=[pl.BlockSpec((samples, width), lambda p: (0, p))] * 2
        + [pl.BlockSpec((width, samples), lambda p: (p, 0))] * 2,
        out_shape=[flat, flat, tall, tall],
        compiler_params=pltpu.CompilerParams(vmem_limit_bytes=16 << 20),
        cost_estimate=SHORT,
        name="split_design",
    )(design, *earlier)


def normal_rows(filter_taps, block_index, epochs, total):
    components, tap_count = filter_taps.shape
    lanes = -(-(total + tap_count) // 128) * 128

    def kernel(index_ref, taps_ref, out_ref, lag_ref):
        for c in range(components):
            row = jnp.concatenate([taps_ref[c : c + 1], jnp.zeros((1, lanes - tap_count), jnp.float32)], axis=1)
            square = jnp.broadcast_to(row, (epochs, lanes))
            for block in range(total // epochs):
                rolled = pltpu.roll(square, block * epochs, 1, stride=1, stride_axis=0)
                lag_ref[block * epochs : (block + 1) * epochs, :] = rolled[:, :total]
            staggered = pltpu.roll(square, 0, 1, stride=1, stride_axis=0)
            weight = pltpu.roll(staggered, index_ref[0] * epochs, 1)[:, :total]
            rows = lax.dot_general(weight, lag_ref[...], ALONG, precision=HIGHEST, preferred_element_type=jnp.float32)
            for block in range(total // epochs):
                out_ref[block, c] = rows[:, block * epochs : (block + 1) * epochs]

    return pl.pallas_call(
        kernel,
        grid_spec=pltpu.PrefetchScalarGridSpec(
            num_scalar_prefetch=1,
            grid=(1,),
            in_specs=[pl.BlockSpec((components, tap_count), lambda c, index: (0, 0))],
            out_specs=pl.BlockSpec((total // epochs, components, epochs, epochs), lambda c, index: (0, 0, 0, 0)),
            scratch_shapes=[pltpu.VMEM((total, total), jnp.float32)],
        ),
        out_shape=jax.ShapeDtypeStruct((total // epochs, components, epochs, epochs), jnp.float32),
        compiler_params=pltpu.CompilerParams(vmem_limit_bytes=(8 << 20) + 6 * total * total),
        cost_estimate=SHORT,
        name="normal_rows",
    )(jnp.reshape(block_index, (1,)).astype(jnp.int32), filter_taps)


def project(tall_high, tall_low, own, chunk, arrivals, shards, tile):
    coefficients, samples = tall_high.shape
    slots = len(arrivals) + 1
    rows = arrivals[0][0].shape[0]
    width = math.gcd(coefficients, 5120)
    counts = [len(pieces) for pieces in arrivals]
    pieces = [piece for group in arrivals for piece in group]

    def kernel(shard_ref, high_ref, low_ref, own_ref, *refs):
        *piece_refs, _, out_ref = refs
        values = [own_ref[...]]
        start = 0
        for count in counts:
            value = piece_refs[start][...]
            for ref in piece_refs[start + 1 : start + count]:
                value = value + ref[...]
            values.append(value)
            start += count
        part = three_passes(jnp.concatenate(values, axis=0), high_ref[...], low_ref[...])

        @pl.when(pl.program_id(0) == 0)
        def _():
            out_ref[...] = jnp.zeros_like(out_ref)

        for slot in range(slots):
            out_ref[shard_ref[slot]] += part[slot * rows : (slot + 1) * rows]

    return pl.pallas_call(
        kernel,
        grid_spec=pltpu.PrefetchScalarGridSpec(
            num_scalar_prefetch=1,
            grid=(coefficients // width,),
            in_specs=[
                pl.BlockSpec((width, samples), lambda p, shard: (p, 0)),
                pl.BlockSpec((width, samples), lambda p, shard: (p, 0)),
                pl.BlockSpec((rows, width), lambda p, shard: (chunk, p)),
            ]
            + [pl.BlockSpec((rows, width), lambda p, shard: (0, p)) for _ in pieces]
            + [pl.BlockSpec(memory_space=pl.ANY)],
            out_specs=pl.BlockSpec((slots, rows, samples), lambda p, shard: (0, 0, 0)),
        ),
        out_shape=jax.ShapeDtypeStruct((slots, rows, samples), jnp.float32),
        compiler_params=pltpu.CompilerParams(vmem_limit_bytes=24 << 20),
        cost_estimate=SHORT,
        name="project",
    )(shards, tall_high, tall_low, own, *pieces, tile)


def multiply(high, low, taps, blocks, places, shards, tile):
    samples, coefficients = high.shape
    _, components, epochs, _ = taps.shape
    slots, rows, _ = blocks[0].shape
    width = math.gcd(coefficients, 5120)
    count = len(blocks)

    def kernel(shard_ref, place_ref, high_ref, low_ref, taps_ref, *refs):
        block_refs = refs[:count]
        out_refs = refs[count + 1 : -1]
        weighted_ref = refs[-1]

        @pl.when(pl.program_id(0) == 0)
        def _():
            sums = [0.0] * components
            for source in range(count):
                block = block_refs[source][...].reshape(slots * rows, samples)
                for c in range(components):
                    piece = block[:, c * epochs : (c + 1) * epochs]
                    factor = taps_ref[place_ref[source], c]
                    sums[c] = sums[c] + lax.dot_general(
                        piece, factor, ALONG, precision=HIGHEST, preferred_element_type=jnp.float32
                    )
            weighted_ref[...] = jnp.concatenate(sums, axis=1).reshape(slots, rows, samples)

        weighted = jnp.concatenate([weighted_ref[shard_ref[slot]] for slot in range(slots)], axis=0)
        product = three_passes(weighted, high_ref[...], low_ref[...])
        for slot in range(slots):
            out_refs[slot][...] = product[slot * rows : (slot + 1) * rows]

    return pl.pallas_call(
        kernel,
        grid_spec=pltpu.PrefetchScalarGridSpec(
            num_scalar_prefetch=2,
            grid=(coefficients // width,),
            in_specs=[
                pl.BlockSpec((samples, width), lambda p, shard, place: (0, p)),
                pl.BlockSpec((samples, width), lambda p, shard, place: (0, p)),
                pl.BlockSpec(taps.shape, lambda p, shard, place: (0, 0, 0, 0)),
            ]
            + [pl.BlockSpec((slots, rows, samples), lambda p, shard, place: (0, 0, 0)) for _ in blocks]
            + [pl.BlockSpec(memory_space=pl.ANY)],
            out_specs=[pl.BlockSpec((rows, width), lambda p, shard, place: (0, p)) for _ in range(slots)],
            scratch_shapes=[pltpu.VMEM((slots, rows, samples), jnp.float32)],
        ),
        out_shape=[jax.ShapeDtypeStruct((rows, coefficients), jnp.float32) for _ in range(slots)],
        compiler_params=pltpu.CompilerParams(vmem_limit_bytes=24 << 20),
        cost_estimate=SHORT,
        name="multiply",
    )(shards, places, high, low, taps, *blocks, tile)


def add_up(shares):
    count, slots, rows, samples = shares.shape

    def kernel(shares_ref, out_ref):
        value = shares_ref[0]
        for share in range(1, count):
            value = value + shares_ref[share]
        out_ref[...] = value

    return pl.pallas_call(
        kernel,
        out_shape=jax.ShapeDtypeStruct((slots, rows, samples), jnp.float32),
        compiler_params=pltpu.CompilerParams(vmem_limit_bytes=8 << 20),
        cost_estimate=SHORT,
        name="add_up",
    )(shares)


def totals_of(groups, tile):
    rows, coefficients = groups[0][0].shape
    width = math.gcd(coefficients, 5120)
    values = [value for group in groups for value in group]

    def kernel(*refs):
        start = 0
        for index, group in enumerate(groups):
            value = refs[start][...]
            for ref in refs[start + 1 : start + len(group)]:
                value = value + ref[...]
            refs[-1][index * rows : (index + 1) * rows, :] = value
            start += len(group)

    return pl.pallas_call(
        kernel,
        grid=(coefficients // width,),
        in_specs=[pl.BlockSpec((rows, width), lambda p: (0, p)) for _ in values] + [pl.BlockSpec(memory_space=pl.ANY)],
        out_specs=pl.BlockSpec((rows * len(groups), width), lambda p: (0, p)),
        out_shape=jax.ShapeDtypeStruct((rows * len(groups), coefficients), jnp.float32),
        compiler_params=pltpu.CompilerParams(vmem_limit_bytes=12 << 20),
        cost_estimate=LONG,
        name="totals_of",
    )(*values, tile)


def step_pairs(length, step, parity):
    pairs = []
    for low in range(parity, length - 1, 2):
        if low - step + 1 >= 0:
            pairs.append((low, low + 1))
        if low + step < length:
            pairs.append((low + 1, low))
    return pairs


def mark(tile, *values):
    count = len(values)

    def kernel(tile_ref, *refs):
        refs[count][...] = tile_ref[...]

    return pl.pallas_call(
        kernel,
        in_specs=[pl.BlockSpec(memory_space=pltpu.VMEM)] + [pl.BlockSpec(memory_space=pl.ANY)] * count,
        out_shape=jax.ShapeDtypeStruct(tile.shape, tile.dtype),
        compiler_params=pltpu.CompilerParams(vmem_limit_bytes=1 << 20),
        cost_estimate=LONG,
        name="mark",
    )(tile, *values)


class Gather:
    def __init__(self, value, length):
        self.length = length
        self.arrived = {(0, 0): value, (1, 0): value}
        self.done = 0

    def step(self, count=1):
        for _ in range(min(count, self.length - 1 - self.done)):
            self.done += 1
            for parity in (0, 1):
                pairs = step_pairs(self.length, self.done, parity)
                if pairs:
                    self.arrived[parity, self.done] = lax.ppermute(self.arrived[1 - parity, self.done - 1], "tm", pairs)

    def tie(self, tile, parities=(0, 1)):
        for parity in parities:
            if (parity, self.done) in self.arrived:
                tile, value = lax.optimization_barrier((tile, self.arrived[parity, self.done]))
                self.arrived[parity, self.done] = value
        return tile

    def slots(self):
        self.step(self.length)
        return [
            [self.arrived[key] for key in ((0, slot), (1, self.length - slot)) if key in self.arrived]
            for slot in range(1, self.length)
        ]


class Reduction:
    def __init__(self, slots, length):
        self.length = length
        self.slots = slots
        self.pending = {}
        self.left = length

    def step(self, count=1):
        for _ in range(min(count, self.left - 1)):
            self.left -= 1
            for parity in (0, 1):
                pairs = step_pairs(self.length, self.left, parity)
                if pairs:
                    value = self.slots[self.left] if parity == 0 else self.slots[self.length - self.left]
                    if (1 - parity, self.left + 1) in self.pending:
                        value = value + self.pending[1 - parity, self.left + 1]
                    self.pending[parity, self.left] = lax.ppermute(value, "tm", [(b, a) for a, b in pairs])

    def tie(self, tile, parities=(0, 1)):
        for parity in parities:
            if (parity, self.left) in self.pending:
                tile, value = lax.optimization_barrier((tile, self.pending[parity, self.left]))
                self.pending[parity, self.left] = value
        return tile

    def addends(self):
        self.step(self.length)
        return [self.slots[0]] + [self.pending[key] for key in ((0, 1), (1, 1)) if key in self.pending]


def is_direct(length):
    return length <= 8 and length & (length - 1) == 0


def places_of(length):
    numbers = jnp.arange(length, dtype=jnp.int32)
    return lax.axis_index("tm") ^ numbers if is_direct(length) else numbers


def exchange(value, length):
    if is_direct(length):
        return [value] + [lax.ppermute(value, "tm", [(i, i ^ by) for i in range(length)]) for by in range(1, length)]
    gathered = lax.all_gather(value, "tm", axis=0)
    return [gathered[i] for i in range(length)]


def body(design, filter_taps, probes):
    components, epochs, coefficients = design.shape
    length = lax.axis_size("tm")
    place = lax.axis_index("tm")
    own = probes.T
    columns = own.shape[0]
    chunks = 2 if columns % 16 == 0 else 1
    rows = columns // chunks
    direction = 1 - 2 * (place % 2)
    shards = (place + direction * jnp.arange(length, dtype=jnp.int32)) % length
    places = places_of(length)
    taps = normal_rows(filter_taps, place, epochs, length * epochs)
    tile = jnp.zeros((8, 128), jnp.float32)
    high, low, tall_high, tall_low = split_design(design, [taps, shards, places, tile])

    def summed(partial):
        return add_up(lax.all_gather(partial, "param", axis=0))

    def multiplied(blocks, tile):
        slots = multiply(high, low, taps, blocks, places, shards, tile)
        tile, *slots = lax.optimization_barrier((tile, *slots))
        return Reduction(slots, length), tile

    first = Gather(own[:rows], length)
    first.step()
    tile, taps, shards, places, high, low = lax.optimization_barrier((tile, taps, shards, places, high, low))
    tile = first.tie(tile)
    first.step()
    if chunks == 1:
        partial = project(tall_high, tall_low, own, 0, first.slots(), shards, tile)
        ahead, tile = multiplied(exchange(summed(partial), length), tile)
        return totals_of([ahead.addends()], tile).T
    tile, value = lax.optimization_barrier((mark(tile), own[rows:]))
    second = Gather(value, length)
    second.step()
    tile = first.tie(tile)
    first.step(length)
    tile = second.tie(mark(tile))
    second.step()
    partial = project(tall_high, tall_low, own, 0, first.slots(), shards, mark(tile))
    projected = summed(partial)
    blocks = exchange(projected, length)
    tile, *blocks = lax.optimization_barrier((tile, *blocks))
    tile = second.tie(tile)
    second.step(length)
    ahead, tile = multiplied(blocks, mark(tile))
    ahead.step()
    partial = project(tall_high, tall_low, own, 1, second.slots(), shards, mark(tile))
    projected = summed(partial)
    blocks = exchange(projected, length)
    tile = ahead.tie(mark(tile, projected), (0,))
    ahead.step()
    trailing, tile = multiplied(blocks, mark(tile))
    trailing.step()
    tile = ahead.tie(mark(tile))
    ahead.step(length)
    tile = trailing.tie(mark(tile), (0,))
    trailing.step()
    tile = trailing.tie(mark(tile))
    trailing.step(length)
    tile = ahead.tie(mark(tile))
    return totals_of([ahead.addends(), trailing.addends()], tile).T


def solution(mesh):
    in_specs = (P(None, ("groups", "tm"), "param"), P(), P("param", ("groups", "tm")))
    out_specs = P("param", ("groups", "tm"))
    return jax.shard_map(body, mesh=mesh, in_specs=in_specs, out_specs=out_specs, check_vma=False)
```

```python
import math

import jax
import jax.numpy as jnp
from jax import lax
from jax.experimental import pallas as pl
from jax.experimental.pallas import tpu as pltpu
from jax.sharding import PartitionSpec as P


def cost(size):
    return pl.CostEstimate(flops=1, bytes_accessed=size, transcendentals=0)


SHORT = cost(1)
LONG = cost(200_000_000)
HIGHEST = lax.Precision.HIGHEST
ALONG = (((1,), (1,)), ((), ()))
ACROSS = (((1,), (0,)), ((), ()))


def split(value):
    high = value.astype(jnp.bfloat16)
    return high, (value - high.astype(jnp.float32)).astype(jnp.bfloat16)


def three_passes(left, right_high, right_low):
    left_high, left_low = split(left)
    height = left.shape[0]
    both = jnp.concatenate([left_high, left_low], axis=0)
    first = lax.dot_general(both, right_high, ACROSS, preferred_element_type=jnp.float32)
    last = lax.dot_general(left_high, right_low, ACROSS, preferred_element_type=jnp.float32)
    return first[:height] + (first[height:] + last)


def split_design(design, earlier):
    components, epochs, coefficients = design.shape
    samples = components * epochs
    width = math.gcd(coefficients, 2048)

    def kernel(design_ref, *refs):
        high_ref, low_ref, tall_high_ref, tall_low_ref = refs[-4:]
        block = design_ref[...].reshape(samples, width)
        high_ref[...], low_ref[...] = split(block)
        tall_high_ref[...], tall_low_ref[...] = split(block.T)

    flat = jax.ShapeDtypeStruct((samples, coefficients), jnp.bfloat16)
    tall = jax.ShapeDtypeStruct((coefficients, samples), jnp.bfloat16)
    return pl.pallas_call(
        kernel,
        grid=(coefficients // width,),
        in_specs=[pl.BlockSpec((components, epochs, width), lambda p: (0, 0, p))]
        + [pl.BlockSpec(memory_space=pl.ANY)] * len(earlier),
        out_specs=[pl.BlockSpec((samples, width), lambda p: (0, p))] * 2
        + [pl.BlockSpec((width, samples), lambda p: (p, 0))] * 2,
        out_shape=[flat, flat, tall, tall],
        compiler_params=pltpu.CompilerParams(vmem_limit_bytes=16 << 20),
        cost_estimate=SHORT,
        name="split_design",
    )(design, *earlier)


def normal_rows(filter_taps, block_index, epochs, total):
    components, tap_count = filter_taps.shape
    lanes = -(-(total + tap_count) // 128) * 128

    def kernel(index_ref, taps_ref, out_ref, lag_ref):
        for c in range(components):
            row = jnp.concatenate([taps_ref[c : c + 1], jnp.zeros((1, lanes - tap_count), jnp.float32)], axis=1)
            square = jnp.broadcast_to(row, (epochs, lanes))
            for block in range(total // epochs):
                rolled = pltpu.roll(square, block * epochs, 1, stride=1, stride_axis=0)
                lag_ref[block * epochs : (block + 1) * epochs, :] = rolled[:, :total]
            staggered = pltpu.roll(square, 0, 1, stride=1, stride_axis=0)
            weight = pltpu.roll(staggered, index_ref[0] * epochs, 1)[:, :total]
            rows = lax.dot_general(weight, lag_ref[...], ALONG, precision=HIGHEST, preferred_element_type=jnp.float32)
            for block in range(total // epochs):
                out_ref[block, c] = rows[:, block * epochs : (block + 1) * epochs]

    return pl.pallas_call(
        kernel,
        grid_spec=pltpu.PrefetchScalarGridSpec(
            num_scalar_prefetch=1,
            grid=(1,),
            in_specs=[pl.BlockSpec((components, tap_count), lambda c, index: (0, 0))],
            out_specs=pl.BlockSpec((total // epochs, components, epochs, epochs), lambda c, index: (0, 0, 0, 0)),
            scratch_shapes=[pltpu.VMEM((total, total), jnp.float32)],
        ),
        out_shape=jax.ShapeDtypeStruct((total // epochs, components, epochs, epochs), jnp.float32),
        compiler_params=pltpu.CompilerParams(vmem_limit_bytes=(8 << 20) + 6 * total * total),
        cost_estimate=SHORT,
        name="normal_rows",
    )(jnp.reshape(block_index, (1,)).astype(jnp.int32), filter_taps)


def project(tall_high, tall_low, own, chunk, arrivals, shards, tile):
    coefficients, samples = tall_high.shape
    slots = len(arrivals) + 1
    rows = arrivals[0][0].shape[0]
    width = math.gcd(coefficients, 5120)
    counts = [len(pieces) for pieces in arrivals]
    pieces = [piece for group in arrivals for piece in group]

    def kernel(shard_ref, high_ref, low_ref, own_ref, *refs):
        *piece_refs, _, out_ref = refs
        values = [own_ref[...]]
        start = 0
        for count in counts:
            value = piece_refs[start][...]
            for ref in piece_refs[start + 1 : start + count]:
                value = value + ref[...]
            values.append(value)
            start += count
        part = three_passes(jnp.concatenate(values, axis=0), high_ref[...], low_ref[...])

        @pl.when(pl.program_id(0) == 0)
        def _():
            out_ref[...] = jnp.zeros_like(out_ref)

        for slot in range(slots):
            out_ref[shard_ref[slot]] += part[slot * rows : (slot + 1) * rows]

    return pl.pallas_call(
        kernel,
        grid_spec=pltpu.PrefetchScalarGridSpec(
            num_scalar_prefetch=1,
            grid=(coefficients // width,),
            in_specs=[
                pl.BlockSpec((width, samples), lambda p, shard: (p, 0)),
                pl.BlockSpec((width, samples), lambda p, shard: (p, 0)),
                pl.BlockSpec((rows, width), lambda p, shard: (chunk, p)),
            ]
            + [pl.BlockSpec((rows, width), lambda p, shard: (0, p)) for _ in pieces]
            + [pl.BlockSpec(memory_space=pl.ANY)],
            out_specs=pl.BlockSpec((slots, rows, samples), lambda p, shard: (0, 0, 0)),
        ),
        out_shape=jax.ShapeDtypeStruct((slots, rows, samples), jnp.float32),
        compiler_params=pltpu.CompilerParams(vmem_limit_bytes=24 << 20),
        cost_estimate=SHORT,
        name="project",
    )(shards, tall_high, tall_low, own, *pieces, tile)


def multiply(high, low, taps, blocks, places, shards, tile):
    samples, coefficients = high.shape
    _, components, epochs, _ = taps.shape
    slots, rows, _ = blocks[0].shape
    width = math.gcd(coefficients, 5120)
    count = len(blocks)

    def kernel(shard_ref, place_ref, high_ref, low_ref, taps_ref, *refs):
        block_refs = refs[:count]
        out_refs = refs[count + 1 : -1]
        weighted_ref = refs[-1]

        @pl.when(pl.program_id(0) == 0)
        def _():
            sums = [0.0] * components
            for source in range(count):
                block = block_refs[source][...].reshape(slots * rows, samples)
                for c in range(components):
                    piece = block[:, c * epochs : (c + 1) * epochs]
                    factor = taps_ref[place_ref[source], c]
                    sums[c] = sums[c] + lax.dot_general(
                        piece, factor, ALONG, precision=HIGHEST, preferred_element_type=jnp.float32
                    )
            weighted_ref[...] = jnp.concatenate(sums, axis=1).reshape(slots, rows, samples)

        weighted = jnp.concatenate([weighted_ref[shard_ref[slot]] for slot in range(slots)], axis=0)
        product = three_passes(weighted, high_ref[...], low_ref[...])
        for slot in range(slots):
            out_refs[slot][...] = product[slot * rows : (slot + 1) * rows]

    return pl.pallas_call(
        kernel,
        grid_spec=pltpu.PrefetchScalarGridSpec(
            num_scalar_prefetch=2,
            grid=(coefficients // width,),
            in_specs=[
                pl.BlockSpec((samples, width), lambda p, shard, place: (0, p)),
                pl.BlockSpec((samples, width), lambda p, shard, place: (0, p)),
                pl.BlockSpec(taps.shape, lambda p, shard, place: (0, 0, 0, 0)),
            ]
            + [pl.BlockSpec((slots, rows, samples), lambda p, shard, place: (0, 0, 0)) for _ in blocks]
            + [pl.BlockSpec(memory_space=pl.ANY)],
            out_specs=[pl.BlockSpec((rows, width), lambda p, shard, place: (0, p)) for _ in range(slots)],
            scratch_shapes=[pltpu.VMEM((slots, rows, samples), jnp.float32)],
        ),
        out_shape=[jax.ShapeDtypeStruct((rows, coefficients), jnp.float32) for _ in range(slots)],
        compiler_params=pltpu.CompilerParams(vmem_limit_bytes=24 << 20),
        cost_estimate=SHORT,
        name="multiply",
    )(shards, places, high, low, taps, *blocks, tile)


def add_up(shares):
    count, slots, rows, samples = shares.shape

    def kernel(shares_ref, out_ref):
        value = shares_ref[0]
        for share in range(1, count):
            value = value + shares_ref[share]
        out_ref[...] = value

    return pl.pallas_call(
        kernel,
        out_shape=jax.ShapeDtypeStruct((slots, rows, samples), jnp.float32),
        compiler_params=pltpu.CompilerParams(vmem_limit_bytes=8 << 20),
        cost_estimate=SHORT,
        name="add_up",
    )(shares)


def totals_of(groups, tile):
    rows, coefficients = groups[0][0].shape
    width = math.gcd(coefficients, 5120)
    values = [value for group in groups for value in group]

    def kernel(*refs):
        start = 0
        for index, group in enumerate(groups):
            value = refs[start][...]
            for ref in refs[start + 1 : start + len(group)]:
                value = value + ref[...]
            refs[-1][index * rows : (index + 1) * rows, :] = value
            start += len(group)

    return pl.pallas_call(
        kernel,
        grid=(coefficients // width,),
        in_specs=[pl.BlockSpec((rows, width), lambda p: (0, p)) for _ in values] + [pl.BlockSpec(memory_space=pl.ANY)],
        out_specs=pl.BlockSpec((rows * len(groups), width), lambda p: (0, p)),
        out_shape=jax.ShapeDtypeStruct((rows * len(groups), coefficients), jnp.float32),
        compiler_params=pltpu.CompilerParams(vmem_limit_bytes=12 << 20),
        cost_estimate=LONG,
        name="totals_of",
    )(*values, tile)


def step_pairs(length, step, parity):
    pairs = []
    for low in range(parity, length - 1, 2):
        if low - step + 1 >= 0:
            pairs.append((low, low + 1))
        if low + step < length:
            pairs.append((low + 1, low))
    return pairs


def mark(tile, *values):
    count = len(values)

    def kernel(tile_ref, *refs):
        refs[count][...] = tile_ref[...]

    return pl.pallas_call(
        kernel,
        in_specs=[pl.BlockSpec(memory_space=pltpu.VMEM)] + [pl.BlockSpec(memory_space=pl.ANY)] * count,
        out_shape=jax.ShapeDtypeStruct(tile.shape, tile.dtype),
        compiler_params=pltpu.CompilerParams(vmem_limit_bytes=1 << 20),
        cost_estimate=LONG,
        name="mark",
    )(tile, *values)


class Gather:
    def __init__(self, value, length):
        self.length = length
        self.onward = {(0, 0): value, (1, 0): value}
        self.arrived = {}

    def pairs(self, parity, step, onward):
        sources = {source for source, _ in step_pairs(self.length, step + 1, 1 - parity)}
        return [pair for pair in step_pairs(self.length, step, parity) if (pair[1] in sources) == onward]

    def send(self, parity, step, kinds=(True, False)):
        pairs = [pair for onward in kinds for pair in self.pairs(parity, step, onward)]
        if pairs:
            value = lax.ppermute(self.onward[1 - parity, step - 1], "tm", pairs)
            self.arrived.setdefault((parity, step), []).append(value)
            if True in kinds:
                self.onward[parity, step] = value

    def tie(self, tile, parity, step):
        values = self.arrived.get((parity, step), [])
        if values:
            places = [index for index, value in enumerate(values) if value is self.onward.get((parity, step))]
            tile, *values = lax.optimization_barrier((tile, *values))
            self.arrived[parity, step] = values
            for index in places:
                self.onward[parity, step] = values[index]
        return tile

    def slots(self):
        return [
            self.arrived.get((0, slot), []) + self.arrived.get((1, self.length - slot), [])
            for slot in range(1, self.length)
        ]


class Reduction:
    def __init__(self, slots, length):
        self.length = length
        self.slots = slots
        self.pending = {}

    def pairs(self, parity, step, free):
        receivers = {source for source, _ in step_pairs(self.length, step + 1, 1 - parity)}
        pairs = [(b, a) for a, b in step_pairs(self.length, step, parity)]
        return [pair for pair in pairs if (pair[0] not in receivers) == free]

    def send(self, parity, step, kinds=(True, False)):
        pairs = [pair for free in kinds for pair in self.pairs(parity, step, free)]
        if pairs:
            value = self.slots[step] if parity == 0 else self.slots[self.length - step]
            if False in kinds:
                for other in self.pending.get((1 - parity, step + 1), []):
                    value = value + other
            self.pending.setdefault((parity, step), []).append(lax.ppermute(value, "tm", pairs))

    def tie(self, tile, parity, step):
        values = self.pending.get((parity, step), [])
        if values:
            tile, *values = lax.optimization_barrier((tile, *values))
            self.pending[parity, step] = values
        return tile

    def addends(self):
        return [self.slots[0]] + self.pending.get((0, 1), []) + self.pending.get((1, 1), [])


def is_direct(length):
    return length <= 8 and length & (length - 1) == 0


def places_of(length):
    numbers = jnp.arange(length, dtype=jnp.int32)
    return lax.axis_index("tm") ^ numbers if is_direct(length) else numbers


def exchange(value, length):
    if is_direct(length):
        return [value] + [lax.ppermute(value, "tm", [(i, i ^ by) for i in range(length)]) for by in range(1, length)]
    gathered = lax.all_gather(value, "tm", axis=0)
    return [gathered[i] for i in range(length)]


def body(design, filter_taps, probes):
    components, epochs, coefficients = design.shape
    length = lax.axis_size("tm")
    place = lax.axis_index("tm")
    own = probes.T
    columns = own.shape[0]
    chunks = 2 if columns % 16 == 0 else 1
    rows = columns // chunks
    direction = 1 - 2 * (place % 2)
    shards = (place + direction * jnp.arange(length, dtype=jnp.int32)) % length
    places = places_of(length)
    taps = normal_rows(filter_taps, place, epochs, length * epochs)
    tile = jnp.zeros((8, 128), jnp.float32)
    high, low, tall_high, tall_low = split_design(design, [taps, shards, places, tile])

    def summed(partial):
        return add_up(lax.all_gather(partial, "param", axis=0))

    def multiplied(blocks, tile):
        slots = multiply(high, low, taps, blocks, places, shards, tile)
        tile, *slots = lax.optimization_barrier((tile, *slots))
        return Reduction(slots, length), tile

    if chunks == 1 or length != 4:
        totals = []
        for chunk in range(chunks):
            gather = Gather(own[chunk * rows : (chunk + 1) * rows], length)
            for step in range(1, length):
                gather.send(0, step)
                gather.send(1, step)
            partial = project(tall_high, tall_low, own, chunk, gather.slots(), shards, tile)
            reduction, tile = multiplied(exchange(summed(partial), length), tile)
            for step in range(length - 1, 0, -1):
                reduction.send(0, step)
                reduction.send(1, step)
            totals.append(reduction.addends())
        return totals_of(totals, tile).T

    first = Gather(own[:rows], length)
    first.send(0, 1)
    first.send(1, 1)
    tile, taps, shards, places, high, low = lax.optimization_barrier((tile, taps, shards, places, high, low))
    tile = first.tie(tile, 0, 1)
    tile = first.tie(tile, 1, 1)
    first.send(0, 2)
    first.send(1, 2)
    tile = first.tie(tile, 1, 2)
    first.send(0, 3)
    tile, value = lax.optimization_barrier((mark(tile), own[rows:]))
    second = Gather(value, length)
    second.send(0, 1)
    second.send(1, 1)
    partial = project(tall_high, tall_low, own, 0, first.slots(), shards, tile)
    projected = summed(partial)
    blocks = exchange(projected, length)
    tile, *blocks = lax.optimization_barrier((tile, *blocks))
    tile = second.tie(tile, 0, 1)
    tile = second.tie(tile, 1, 1)
    second.send(0, 2)
    second.send(1, 2)
    ahead, tile = multiplied(blocks, mark(tile))
    ahead.send(0, 3)
    ahead.send(0, 1, (True,))
    tile = second.tie(tile, 0, 2)
    tile = second.tie(tile, 1, 2)
    second.send(0, 3)
    tile = ahead.tie(mark(tile), 0, 3)
    ahead.send(0, 2)
    ahead.send(1, 2)
    partial = project(tall_high, tall_low, own, 1, second.slots(), shards, mark(tile))
    projected = summed(partial)
    blocks = exchange(projected, length)
    tile = ahead.tie(mark(tile, projected), 0, 2)
    tile = ahead.tie(tile, 1, 2)
    ahead.send(0, 1, (False,))
    ahead.send(1, 1)
    free = ahead.pending[0, 1][:1]
    tile, *free = lax.optimization_barrier((tile, *free))
    ahead.pending[0, 1][:1] = free
    trailing, tile = multiplied(blocks, mark(tile))
    trailing.send(0, 3)
    tile = ahead.tie(mark(tile), 0, 1)
    tile = ahead.tie(tile, 1, 1)
    tile, later = lax.optimization_barrier((tile, trailing.slots[2]))
    tile = mark(tile)
    tile = trailing.tie(tile, 0, 3)
    trailing.send(1, 2)
    trailing.slots[2] = later
    trailing.send(0, 2)
    trailing.send(0, 1)
    trailing.send(1, 1)
    return totals_of([ahead.addends(), trailing.addends()], tile).T


def solution(mesh):
    in_specs = (P(None, ("groups", "tm"), "param"), P(), P("param", ("groups", "tm")))
    out_specs = P("param", ("groups", "tm"))
    return jax.shard_map(body, mesh=mesh, in_specs=in_specs, out_specs=out_specs, check_vma=False)
```

```python
import math

import jax
import jax.numpy as jnp
from jax import lax
from jax.experimental import pallas as pl
from jax.experimental.pallas import tpu as pltpu
from jax.sharding import PartitionSpec as P


def cost(size):
    return pl.CostEstimate(flops=1, bytes_accessed=size, transcendentals=0)


SHORT = cost(1)
LONG = cost(200_000_000)
HIGHEST = lax.Precision.HIGHEST
ALONG = (((1,), (1,)), ((), ()))
ACROSS = (((1,), (0,)), ((), ()))


def split(value):
    high = value.astype(jnp.bfloat16)
    return high, (value - high.astype(jnp.float32)).astype(jnp.bfloat16)


def three_passes(left, right_high, right_low, dimensions=ACROSS):
    left_high, left_low = split(left)
    height = left.shape[0]
    both = jnp.concatenate([left_high, left_low], axis=0)
    first = lax.dot_general(both, right_high, dimensions, preferred_element_type=jnp.float32)
    last = lax.dot_general(left_high, right_low, dimensions, preferred_element_type=jnp.float32)
    return first[:height] + (first[height:] + last)


def split_design(design, earlier):
    components, epochs, coefficients = design.shape
    samples = components * epochs
    width = math.gcd(coefficients, 2048)

    def kernel(design_ref, *refs):
        high_ref, low_ref, tall_high_ref, tall_low_ref = refs[-4:]
        block = design_ref[...].reshape(samples, width)
        high_ref[...], low_ref[...] = split(block)
        tall_high_ref[...], tall_low_ref[...] = split(block.T)

    flat = jax.ShapeDtypeStruct((samples, coefficients), jnp.bfloat16)
    tall = jax.ShapeDtypeStruct((coefficients, samples), jnp.bfloat16)
    return pl.pallas_call(
        kernel,
        grid=(coefficients // width,),
        in_specs=[pl.BlockSpec((components, epochs, width), lambda p: (0, 0, p))]
        + [pl.BlockSpec(memory_space=pl.ANY)] * len(earlier),
        out_specs=[pl.BlockSpec((samples, width), lambda p: (0, p))] * 2
        + [pl.BlockSpec((width, samples), lambda p: (p, 0))] * 2,
        out_shape=[flat, flat, tall, tall],
        compiler_params=pltpu.CompilerParams(vmem_limit_bytes=16 << 20),
        cost_estimate=SHORT,
        name="split_design",
    )(design, *earlier)


def normal_rows(filter_taps, block_index, epochs, total):
    components, tap_count = filter_taps.shape
    lanes = -(-(total + tap_count) // 128) * 128

    def kernel(index_ref, taps_ref, out_ref, lag_ref):
        for c in range(components):
            row = jnp.concatenate([taps_ref[c : c + 1], jnp.zeros((1, lanes - tap_count), jnp.float32)], axis=1)
            square = jnp.broadcast_to(row, (epochs, lanes))
            for block in range(total // epochs):
                rolled = pltpu.roll(square, block * epochs, 1, stride=1, stride_axis=0)
                lag_ref[block * epochs : (block + 1) * epochs, :] = rolled[:, :total]
            staggered = pltpu.roll(square, 0, 1, stride=1, stride_axis=0)
            weight = pltpu.roll(staggered, index_ref[0] * epochs, 1)[:, :total]
            rows = lax.dot_general(weight, lag_ref[...], ALONG, precision=HIGHEST, preferred_element_type=jnp.float32)
            for block in range(total // epochs):
                out_ref[block, c] = rows[:, block * epochs : (block + 1) * epochs]

    return pl.pallas_call(
        kernel,
        grid_spec=pltpu.PrefetchScalarGridSpec(
            num_scalar_prefetch=1,
            grid=(1,),
            in_specs=[pl.BlockSpec((components, tap_count), lambda c, index: (0, 0))],
            out_specs=pl.BlockSpec((total // epochs, components, epochs, epochs), lambda c, index: (0, 0, 0, 0)),
            scratch_shapes=[pltpu.VMEM((total, total), jnp.float32)],
        ),
        out_shape=jax.ShapeDtypeStruct((total // epochs, components, epochs, epochs), jnp.float32),
        compiler_params=pltpu.CompilerParams(vmem_limit_bytes=(8 << 20) + 6 * total * total),
        cost_estimate=SHORT,
        name="normal_rows",
    )(jnp.reshape(block_index, (1,)).astype(jnp.int32), filter_taps)


def project(tall_high, tall_low, own, chunk, arrivals, shards, tile):
    coefficients, samples = tall_high.shape
    slots = len(arrivals) + 1
    rows = arrivals[0][0].shape[0]
    width = math.gcd(coefficients, 5120)
    counts = [len(pieces) for pieces in arrivals]
    pieces = [piece for group in arrivals for piece in group]

    def kernel(shard_ref, high_ref, low_ref, own_ref, *refs):
        *piece_refs, _, out_ref = refs
        values = [own_ref[...]]
        start = 0
        for count in counts:
            value = piece_refs[start][...]
            for ref in piece_refs[start + 1 : start + count]:
                value = value + ref[...]
            values.append(value)
            start += count
        part = three_passes(jnp.concatenate(values, axis=0), high_ref[...], low_ref[...])

        @pl.when(pl.program_id(0) == 0)
        def _():
            out_ref[...] = jnp.zeros_like(out_ref)

        for slot in range(slots):
            out_ref[shard_ref[slot]] += part[slot * rows : (slot + 1) * rows]

    return pl.pallas_call(
        kernel,
        grid_spec=pltpu.PrefetchScalarGridSpec(
            num_scalar_prefetch=1,
            grid=(coefficients // width,),
            in_specs=[
                pl.BlockSpec((width, samples), lambda p, shard: (p, 0)),
                pl.BlockSpec((width, samples), lambda p, shard: (p, 0)),
                pl.BlockSpec((rows, width), lambda p, shard: (chunk, p)),
            ]
            + [pl.BlockSpec((rows, width), lambda p, shard: (0, p)) for _ in pieces]
            + [pl.BlockSpec(memory_space=pl.ANY)],
            out_specs=pl.BlockSpec((slots, rows, samples), lambda p, shard: (0, 0, 0)),
        ),
        out_shape=jax.ShapeDtypeStruct((slots, rows, samples), jnp.float32),
        compiler_params=pltpu.CompilerParams(vmem_limit_bytes=24 << 20),
        cost_estimate=SHORT,
        name="project",
    )(shards, tall_high, tall_low, own, *pieces, tile)


def multiply(high, low, taps, blocks, places, shards, tile):
    samples, coefficients = high.shape
    _, components, epochs, _ = taps.shape
    slots, rows, _ = blocks[0].shape
    width = math.gcd(coefficients, 5120)
    count = len(blocks)

    def kernel(shard_ref, place_ref, high_ref, low_ref, taps_ref, *refs):
        block_refs = refs[:count]
        out_refs = refs[count + 1 : -1]
        weighted_ref = refs[-1]

        @pl.when(pl.program_id(0) == 0)
        def _():
            sums = [0.0] * components
            for source in range(count):
                block = block_refs[source][...].reshape(slots * rows, samples)
                for c in range(components):
                    piece = block[:, c * epochs : (c + 1) * epochs]
                    factor = taps_ref[place_ref[source], c]
                    sums[c] = sums[c] + three_passes(piece, *split(factor), ALONG)
            weighted_ref[...] = jnp.concatenate(sums, axis=1).reshape(slots, rows, samples)

        weighted = jnp.concatenate([weighted_ref[shard_ref[slot]] for slot in range(slots)], axis=0)
        product = three_passes(weighted, high_ref[...], low_ref[...])
        for slot in range(slots):
            out_refs[slot][...] = product[slot * rows : (slot + 1) * rows]

    return pl.pallas_call(
        kernel,
        grid_spec=pltpu.PrefetchScalarGridSpec(
            num_scalar_prefetch=2,
            grid=(coefficients // width,),
            in_specs=[
                pl.BlockSpec((samples, width), lambda p, shard, place: (0, p)),
                pl.BlockSpec((samples, width), lambda p, shard, place: (0, p)),
                pl.BlockSpec(taps.shape, lambda p, shard, place: (0, 0, 0, 0)),
            ]
            + [pl.BlockSpec((slots, rows, samples), lambda p, shard, place: (0, 0, 0)) for _ in blocks]
            + [pl.BlockSpec(memory_space=pl.ANY)],
            out_specs=[pl.BlockSpec((rows, width), lambda p, shard, place: (0, p)) for _ in range(slots)],
            scratch_shapes=[pltpu.VMEM((slots, rows, samples), jnp.float32)],
        ),
        out_shape=[jax.ShapeDtypeStruct((rows, coefficients), jnp.float32) for _ in range(slots)],
        compiler_params=pltpu.CompilerParams(vmem_limit_bytes=24 << 20),
        cost_estimate=SHORT,
        name="multiply",
    )(shards, places, high, low, taps, *blocks, tile)


def add_up(shares):
    count, slots, rows, samples = shares.shape

    def kernel(shares_ref, out_ref):
        value = shares_ref[0]
        for share in range(1, count):
            value = value + shares_ref[share]
        out_ref[...] = value

    return pl.pallas_call(
        kernel,
        out_shape=jax.ShapeDtypeStruct((slots, rows, samples), jnp.float32),
        compiler_params=pltpu.CompilerParams(vmem_limit_bytes=8 << 20),
        cost_estimate=SHORT,
        name="add_up",
    )(shares)


def totals_of(groups, tile):
    rows, coefficients = groups[0][0].shape
    width = math.gcd(coefficients, 5120)
    values = [value for group in groups for value in group]

    def kernel(*refs):
        start = 0
        for index, group in enumerate(groups):
            value = refs[start][...]
            for ref in refs[start + 1 : start + len(group)]:
                value = value + ref[...]
            refs[-1][index * rows : (index + 1) * rows, :] = value
            start += len(group)

    return pl.pallas_call(
        kernel,
        grid=(coefficients // width,),
        in_specs=[pl.BlockSpec((rows, width), lambda p: (0, p)) for _ in values] + [pl.BlockSpec(memory_space=pl.ANY)],
        out_specs=pl.BlockSpec((rows * len(groups), width), lambda p: (0, p)),
        out_shape=jax.ShapeDtypeStruct((rows * len(groups), coefficients), jnp.float32),
        compiler_params=pltpu.CompilerParams(vmem_limit_bytes=12 << 20),
        cost_estimate=LONG,
        name="totals_of",
    )(*values, tile)


def step_pairs(length, step, parity):
    pairs = []
    for low in range(parity, length - 1, 2):
        if low - step + 1 >= 0:
            pairs.append((low, low + 1))
        if low + step < length:
            pairs.append((low + 1, low))
    return pairs


def mark(tile, *values):
    count = len(values)

    def kernel(tile_ref, *refs):
        refs[count][...] = tile_ref[...]

    return pl.pallas_call(
        kernel,
        in_specs=[pl.BlockSpec(memory_space=pltpu.VMEM)] + [pl.BlockSpec(memory_space=pl.ANY)] * count,
        out_shape=jax.ShapeDtypeStruct(tile.shape, tile.dtype),
        compiler_params=pltpu.CompilerParams(vmem_limit_bytes=1 << 20),
        cost_estimate=LONG,
        name="mark",
    )(tile, *values)


class Gather:
    def __init__(self, value, length):
        self.length = length
        self.onward = {(0, 0): value, (1, 0): value}
        self.arrived = {}

    def pairs(self, parity, step, onward):
        sources = {source for source, _ in step_pairs(self.length, step + 1, 1 - parity)}
        return [pair for pair in step_pairs(self.length, step, parity) if (pair[1] in sources) == onward]

    def send(self, parity, step, kinds=(True, False)):
        pairs = [pair for onward in kinds for pair in self.pairs(parity, step, onward)]
        if pairs:
            value = lax.ppermute(self.onward[1 - parity, step - 1], "tm", pairs)
            self.arrived.setdefault((parity, step), []).append(value)
            if True in kinds:
                self.onward[parity, step] = value

    def tie(self, tile, parity, step):
        values = self.arrived.get((parity, step), [])
        if values:
            places = [index for index, value in enumerate(values) if value is self.onward.get((parity, step))]
            tile, *values = lax.optimization_barrier((tile, *values))
            self.arrived[parity, step] = values
            for index in places:
                self.onward[parity, step] = values[index]
        return tile

    def slots(self):
        return [
            self.arrived.get((0, slot), []) + self.arrived.get((1, self.length - slot), [])
            for slot in range(1, self.length)
        ]


class Reduction:
    def __init__(self, slots, length):
        self.length = length
        self.slots = slots
        self.pending = {}

    def pairs(self, parity, step, free):
        receivers = {source for source, _ in step_pairs(self.length, step + 1, 1 - parity)}
        pairs = [(b, a) for a, b in step_pairs(self.length, step, parity)]
        return [pair for pair in pairs if (pair[0] not in receivers) == free]

    def send(self, parity, step, kinds=(True, False)):
        pairs = [pair for free in kinds for pair in self.pairs(parity, step, free)]
        if pairs:
            value = self.slots[step] if parity == 0 else self.slots[self.length - step]
            if False in kinds:
                for other in self.pending.get((1 - parity, step + 1), []):
                    value = value + other
            self.pending.setdefault((parity, step), []).append(lax.ppermute(value, "tm", pairs))

    def tie(self, tile, parity, step):
        values = self.pending.get((parity, step), [])
        if values:
            tile, *values = lax.optimization_barrier((tile, *values))
            self.pending[parity, step] = values
        return tile

    def addends(self):
        return [self.slots[0]] + self.pending.get((0, 1), []) + self.pending.get((1, 1), [])


def is_direct(length):
    return length <= 8 and length & (length - 1) == 0


def places_of(length):
    numbers = jnp.arange(length, dtype=jnp.int32)
    return lax.axis_index("tm") ^ numbers if is_direct(length) else numbers


def exchange(value, length):
    if is_direct(length):
        return [value] + [lax.ppermute(value, "tm", [(i, i ^ by) for i in range(length)]) for by in range(1, length)]
    gathered = lax.all_gather(value, "tm", axis=0)
    return [gathered[i] for i in range(length)]


def body(design, filter_taps, probes):
    components, epochs, coefficients = design.shape
    length = lax.axis_size("tm")
    place = lax.axis_index("tm")
    own = probes.T
    columns = own.shape[0]
    chunks = 2 if columns % 16 == 0 else 1
    rows = columns // chunks
    direction = 1 - 2 * (place % 2)
    shards = (place + direction * jnp.arange(length, dtype=jnp.int32)) % length
    places = places_of(length)
    taps = normal_rows(filter_taps, place, epochs, length * epochs)
    tile = jnp.zeros((8, 128), jnp.float32)

    def summed(partial):
        return add_up(lax.all_gather(partial, "param", axis=0))

    def multiplied(blocks, tile):
        slots = multiply(high, low, taps, blocks, places, shards, tile)
        tile, *slots = lax.optimization_barrier((tile, *slots))
        return Reduction(slots, length), tile

    if chunks == 1 or length != 4:
        high, low, tall_high, tall_low = split_design(design, [taps, shards, places, tile])
        totals = []
        for chunk in range(chunks):
            gather = Gather(own[chunk * rows : (chunk + 1) * rows], length)
            for step in range(1, length):
                gather.send(0, step)
                gather.send(1, step)
            partial = project(tall_high, tall_low, own, chunk, gather.slots(), shards, tile)
            reduction, tile = multiplied(exchange(summed(partial), length), tile)
            for step in range(length - 1, 0, -1):
                reduction.send(0, step)
                reduction.send(1, step)
            totals.append(reduction.addends())
        return totals_of(totals, tile).T

    first = Gather(own[:rows], length)
    first.send(1, 1)
    first.send(0, 1)
    tile, taps, shards, places = lax.optimization_barrier((tile, taps, shards, places))
    tile = first.tie(tile, 0, 1)
    tile = first.tie(tile, 1, 1)
    first.send(0, 2)
    first.send(1, 2)
    tile = first.tie(tile, 1, 2)
    first.send(0, 3)
    high, low, tall_high, tall_low = split_design(design, [taps, shards, places, mark(tile)])
    tile, high, low, value = lax.optimization_barrier((tile, high, low, own[rows:]))
    second = Gather(value, length)
    second.send(0, 1)
    second.send(1, 1)
    partial = project(tall_high, tall_low, own, 0, first.slots(), shards, tile)
    projected = summed(partial)
    blocks = exchange(projected, length)
    tile, *blocks = lax.optimization_barrier((tile, *blocks))
    tile = second.tie(tile, 0, 1)
    tile = second.tie(tile, 1, 1)
    second.send(0, 2)
    second.send(1, 2)
    ahead, tile = multiplied(blocks, mark(tile))
    ahead.send(0, 3)
    ahead.send(0, 1, (True,))
    tile = second.tie(tile, 0, 2)
    tile = second.tie(tile, 1, 2)
    second.send(0, 3)
    tile = ahead.tie(mark(tile), 0, 3)
    ahead.send(0, 2)
    ahead.send(1, 2)
    partial = project(tall_high, tall_low, own, 1, second.slots(), shards, mark(tile))
    projected = summed(partial)
    blocks = exchange(projected, length)
    tile = ahead.tie(mark(tile, projected), 0, 2)
    tile = ahead.tie(tile, 1, 2)
    ahead.send(0, 1, (False,))
    ahead.send(1, 1)
    free = ahead.pending[0, 1][:1]
    tile, *free = lax.optimization_barrier((tile, *free))
    ahead.pending[0, 1][:1] = free
    trailing, tile = multiplied(blocks, mark(tile))
    trailing.send(0, 3)
    tile = ahead.tie(mark(tile), 0, 1)
    tile = ahead.tie(tile, 1, 1)
    tile, later = lax.optimization_barrier((tile, trailing.slots[2]))
    tile = mark(tile)
    tile = trailing.tie(tile, 0, 3)
    trailing.send(1, 2)
    trailing.slots[2] = later
    trailing.send(0, 2)
    trailing.send(0, 1)
    trailing.send(1, 1)
    return totals_of([ahead.addends(), trailing.addends()], tile).T


def solution(mesh):
    in_specs = (P(None, ("groups", "tm"), "param"), P(), P("param", ("groups", "tm")))
    out_specs = P("param", ("groups", "tm"))
    return jax.shard_map(body, mesh=mesh, in_specs=in_specs, out_specs=out_specs, check_vma=False)
```

```python
import math

import jax
import jax.numpy as jnp
from jax import lax
from jax.experimental import pallas as pl
from jax.experimental.pallas import tpu as pltpu
from jax.sharding import PartitionSpec as P


def cost(size):
    return pl.CostEstimate(flops=1, bytes_accessed=size, transcendentals=0)


SHORT = cost(1)
LONG = cost(200_000_000)
HIGHEST = lax.Precision.HIGHEST
ALONG = (((1,), (1,)), ((), ()))
ACROSS = (((1,), (0,)), ((), ()))


def split(value):
    high = value.astype(jnp.bfloat16)
    return high, (value - high.astype(jnp.float32)).astype(jnp.bfloat16)


def three_passes(left, right_high, right_low, dimensions=ACROSS):
    left_high, left_low = split(left)
    height = left.shape[0]
    both = jnp.concatenate([left_high, left_low], axis=0)
    first = lax.dot_general(both, right_high, dimensions, preferred_element_type=jnp.float32)
    last = lax.dot_general(left_high, right_low, dimensions, preferred_element_type=jnp.float32)
    return first[:height] + (first[height:] + last)


def split_design(design, earlier):
    components, epochs, coefficients = design.shape
    samples = components * epochs
    width = math.gcd(coefficients, 2048)

    def kernel(design_ref, *refs):
        high_ref, low_ref, tall_high_ref, tall_low_ref = refs[-4:]
        block = design_ref[...].reshape(samples, width)
        high_ref[...], low_ref[...] = split(block)
        tall_high_ref[...], tall_low_ref[...] = split(block.T)

    flat = jax.ShapeDtypeStruct((samples, coefficients), jnp.bfloat16)
    tall = jax.ShapeDtypeStruct((coefficients, samples), jnp.bfloat16)
    return pl.pallas_call(
        kernel,
        grid=(coefficients // width,),
        in_specs=[pl.BlockSpec((components, epochs, width), lambda p: (0, 0, p))]
        + [pl.BlockSpec(memory_space=pl.ANY)] * len(earlier),
        out_specs=[pl.BlockSpec((samples, width), lambda p: (0, p))] * 2
        + [pl.BlockSpec((width, samples), lambda p: (p, 0))] * 2,
        out_shape=[flat, flat, tall, tall],
        compiler_params=pltpu.CompilerParams(vmem_limit_bytes=16 << 20),
        cost_estimate=SHORT,
        name="split_design",
    )(design, *earlier)


def normal_rows(filter_taps, block_index, epochs, total):
    components, tap_count = filter_taps.shape
    lanes = -(-(total + tap_count) // 128) * 128

    def kernel(index_ref, taps_ref, out_ref, lag_ref):
        for c in range(components):
            row = jnp.concatenate([taps_ref[c : c + 1], jnp.zeros((1, lanes - tap_count), jnp.float32)], axis=1)
            square = jnp.broadcast_to(row, (epochs, lanes))
            for block in range(total // epochs):
                rolled = pltpu.roll(square, block * epochs, 1, stride=1, stride_axis=0)
                lag_ref[block * epochs : (block + 1) * epochs, :] = rolled[:, :total]
            staggered = pltpu.roll(square, 0, 1, stride=1, stride_axis=0)
            weight = pltpu.roll(staggered, index_ref[0] * epochs, 1)[:, :total]
            rows = lax.dot_general(weight, lag_ref[...], ALONG, precision=HIGHEST, preferred_element_type=jnp.float32)
            for block in range(total // epochs):
                out_ref[block, c] = rows[:, block * epochs : (block + 1) * epochs]

    return pl.pallas_call(
        kernel,
        grid_spec=pltpu.PrefetchScalarGridSpec(
            num_scalar_prefetch=1,
            grid=(1,),
            in_specs=[pl.BlockSpec((components, tap_count), lambda c, index: (0, 0))],
            out_specs=pl.BlockSpec((total // epochs, components, epochs, epochs), lambda c, index: (0, 0, 0, 0)),
            scratch_shapes=[pltpu.VMEM((total, total), jnp.float32)],
        ),
        out_shape=jax.ShapeDtypeStruct((total // epochs, components, epochs, epochs), jnp.float32),
        compiler_params=pltpu.CompilerParams(vmem_limit_bytes=(8 << 20) + 6 * total * total),
        cost_estimate=SHORT,
        name="normal_rows",
    )(jnp.reshape(block_index, (1,)).astype(jnp.int32), filter_taps)


def project(tall_high, tall_low, own, chunk, arrivals, shards, tile):
    coefficients, samples = tall_high.shape
    slots = len(arrivals) + 1
    rows = arrivals[0][0].shape[0]
    width = math.gcd(coefficients, 10240)
    counts = [len(pieces) for pieces in arrivals]
    pieces = [piece for group in arrivals for piece in group]

    def kernel(shard_ref, high_ref, low_ref, own_ref, *refs):
        *piece_refs, _, out_ref = refs
        values = [own_ref[...]]
        start = 0
        for count in counts:
            value = piece_refs[start][...]
            for ref in piece_refs[start + 1 : start + count]:
                value = value + ref[...]
            values.append(value)
            start += count
        part = three_passes(jnp.concatenate(values, axis=0), high_ref[...], low_ref[...])

        @pl.when(pl.program_id(0) == 0)
        def _():
            out_ref[...] = jnp.zeros_like(out_ref)

        for slot in range(slots):
            out_ref[shard_ref[slot]] += part[slot * rows : (slot + 1) * rows]

    return pl.pallas_call(
        kernel,
        grid_spec=pltpu.PrefetchScalarGridSpec(
            num_scalar_prefetch=1,
            grid=(coefficients // width,),
            in_specs=[
                pl.BlockSpec((width, samples), lambda p, shard: (p, 0)),
                pl.BlockSpec((width, samples), lambda p, shard: (p, 0)),
                pl.BlockSpec((rows, width), lambda p, shard: (chunk, p)),
            ]
            + [pl.BlockSpec((rows, width), lambda p, shard: (0, p)) for _ in pieces]
            + [pl.BlockSpec(memory_space=pl.ANY)],
            out_specs=pl.BlockSpec((slots, rows, samples), lambda p, shard: (0, 0, 0)),
        ),
        out_shape=jax.ShapeDtypeStruct((slots, rows, samples), jnp.float32),
        compiler_params=pltpu.CompilerParams(vmem_limit_bytes=24 << 20),
        cost_estimate=SHORT,
        name="project",
    )(shards, tall_high, tall_low, own, *pieces, tile)


def multiply(high, low, taps, blocks, places, shards, tile):
    samples, coefficients = high.shape
    _, components, epochs, _ = taps.shape
    slots, rows, _ = blocks[0].shape
    width = math.gcd(coefficients, 10240)
    count = len(blocks)

    def kernel(shard_ref, place_ref, high_ref, low_ref, taps_ref, *refs):
        block_refs = refs[:count]
        out_refs = refs[count + 1 : -1]
        weighted_ref = refs[-1]

        @pl.when(pl.program_id(0) == 0)
        def _():
            sums = [0.0] * components
            for source in range(count):
                block = block_refs[source][...].reshape(slots * rows, samples)
                for c in range(components):
                    piece = block[:, c * epochs : (c + 1) * epochs]
                    factor = taps_ref[place_ref[source], c]
                    sums[c] = sums[c] + three_passes(piece, *split(factor), ALONG)
            weighted_ref[...] = jnp.concatenate(sums, axis=1).reshape(slots, rows, samples)

        weighted = jnp.concatenate([weighted_ref[shard_ref[slot]] for slot in range(slots)], axis=0)
        product = three_passes(weighted, high_ref[...], low_ref[...])
        for slot in range(slots):
            out_refs[slot][...] = product[slot * rows : (slot + 1) * rows]

    return pl.pallas_call(
        kernel,
        grid_spec=pltpu.PrefetchScalarGridSpec(
            num_scalar_prefetch=2,
            grid=(coefficients // width,),
            in_specs=[
                pl.BlockSpec((samples, width), lambda p, shard, place: (0, p)),
                pl.BlockSpec((samples, width), lambda p, shard, place: (0, p)),
                pl.BlockSpec(taps.shape, lambda p, shard, place: (0, 0, 0, 0)),
            ]
            + [pl.BlockSpec((slots, rows, samples), lambda p, shard, place: (0, 0, 0)) for _ in blocks]
            + [pl.BlockSpec(memory_space=pl.ANY)],
            out_specs=[pl.BlockSpec((rows, width), lambda p, shard, place: (0, p)) for _ in range(slots)],
            scratch_shapes=[pltpu.VMEM((slots, rows, samples), jnp.float32)],
        ),
        out_shape=[jax.ShapeDtypeStruct((rows, coefficients), jnp.float32) for _ in range(slots)],
        compiler_params=pltpu.CompilerParams(vmem_limit_bytes=24 << 20),
        cost_estimate=SHORT,
        name="multiply",
    )(shards, places, high, low, taps, *blocks, tile)


def add_up(shares):
    count, slots, rows, samples = shares.shape

    def kernel(shares_ref, out_ref):
        value = shares_ref[0]
        for share in range(1, count):
            value = value + shares_ref[share]
        out_ref[...] = value

    return pl.pallas_call(
        kernel,
        out_shape=jax.ShapeDtypeStruct((slots, rows, samples), jnp.float32),
        compiler_params=pltpu.CompilerParams(vmem_limit_bytes=8 << 20),
        cost_estimate=SHORT,
        name="add_up",
    )(shares)


def totals_of(groups, tile):
    rows, coefficients = groups[0][0].shape
    width = math.gcd(coefficients, 5120)
    values = [value for group in groups for value in group]

    def kernel(*refs):
        start = 0
        for index, group in enumerate(groups):
            value = refs[start][...]
            for ref in refs[start + 1 : start + len(group)]:
                value = value + ref[...]
            refs[-1][index * rows : (index + 1) * rows, :] = value
            start += len(group)

    return pl.pallas_call(
        kernel,
        grid=(coefficients // width,),
        in_specs=[pl.BlockSpec((rows, width), lambda p: (0, p)) for _ in values] + [pl.BlockSpec(memory_space=pl.ANY)],
        out_specs=pl.BlockSpec((rows * len(groups), width), lambda p: (0, p)),
        out_shape=jax.ShapeDtypeStruct((rows * len(groups), coefficients), jnp.float32),
        compiler_params=pltpu.CompilerParams(vmem_limit_bytes=12 << 20),
        cost_estimate=LONG,
        name="totals_of",
    )(*values, tile)


def step_pairs(length, step, parity):
    pairs = []
    for low in range(parity, length - 1, 2):
        if low - step + 1 >= 0:
            pairs.append((low, low + 1))
        if low + step < length:
            pairs.append((low + 1, low))
    return pairs


def mark(tile, *values):
    count = len(values)

    def kernel(tile_ref, *refs):
        refs[count][...] = tile_ref[...]

    return pl.pallas_call(
        kernel,
        in_specs=[pl.BlockSpec(memory_space=pltpu.VMEM)] + [pl.BlockSpec(memory_space=pl.ANY)] * count,
        out_shape=jax.ShapeDtypeStruct(tile.shape, tile.dtype),
        compiler_params=pltpu.CompilerParams(vmem_limit_bytes=1 << 20),
        cost_estimate=LONG,
        name="mark",
    )(tile, *values)


class Gather:
    def __init__(self, value, length):
        self.length = length
        self.onward = {(0, 0): value, (1, 0): value}
        self.arrived = {}

    def pairs(self, parity, step, onward):
        sources = {source for source, _ in step_pairs(self.length, step + 1, 1 - parity)}
        return [pair for pair in step_pairs(self.length, step, parity) if (pair[1] in sources) == onward]

    def send(self, parity, step, kinds=(True, False)):
        pairs = [pair for onward in kinds for pair in self.pairs(parity, step, onward)]
        if pairs:
            value = lax.ppermute(self.onward[1 - parity, step - 1], "tm", pairs)
            self.arrived.setdefault((parity, step), []).append(value)
            if True in kinds:
                self.onward[parity, step] = value

    def tie(self, tile, parity, step):
        values = self.arrived.get((parity, step), [])
        if values:
            places = [index for index, value in enumerate(values) if value is self.onward.get((parity, step))]
            tile, *values = lax.optimization_barrier((tile, *values))
            self.arrived[parity, step] = values
            for index in places:
                self.onward[parity, step] = values[index]
        return tile

    def slots(self):
        return [
            self.arrived.get((0, slot), []) + self.arrived.get((1, self.length - slot), [])
            for slot in range(1, self.length)
        ]


class Reduction:
    def __init__(self, slots, length):
        self.length = length
        self.slots = slots
        self.pending = {}

    def pairs(self, parity, step, free):
        receivers = {source for source, _ in step_pairs(self.length, step + 1, 1 - parity)}
        pairs = [(b, a) for a, b in step_pairs(self.length, step, parity)]
        return [pair for pair in pairs if (pair[0] not in receivers) == free]

    def send(self, parity, step, kinds=(True, False)):
        pairs = [pair for free in kinds for pair in self.pairs(parity, step, free)]
        if pairs:
            value = self.slots[step] if parity == 0 else self.slots[self.length - step]
            if False in kinds:
                for other in self.pending.get((1 - parity, step + 1), []):
                    value = value + other
            self.pending.setdefault((parity, step), []).append(lax.ppermute(value, "tm", pairs))

    def tie(self, tile, parity, step):
        values = self.pending.get((parity, step), [])
        if values:
            tile, *values = lax.optimization_barrier((tile, *values))
            self.pending[parity, step] = values
        return tile

    def addends(self):
        return [self.slots[0]] + self.pending.get((0, 1), []) + self.pending.get((1, 1), [])


def is_direct(length):
    return length <= 8 and length & (length - 1) == 0


def places_of(length):
    numbers = jnp.arange(length, dtype=jnp.int32)
    return lax.axis_index("tm") ^ numbers if is_direct(length) else numbers


def exchange(value, length):
    if is_direct(length):
        return [value] + [lax.ppermute(value, "tm", [(i, i ^ by) for i in range(length)]) for by in range(1, length)]
    gathered = lax.all_gather(value, "tm", axis=0)
    return [gathered[i] for i in range(length)]


def body(design, filter_taps, probes):
    components, epochs, coefficients = design.shape
    length = lax.axis_size("tm")
    place = lax.axis_index("tm")
    own = probes.T
    columns = own.shape[0]
    chunks = 2 if columns % 16 == 0 else 1
    rows = columns // chunks
    direction = 1 - 2 * (place % 2)
    shards = (place + direction * jnp.arange(length, dtype=jnp.int32)) % length
    places = places_of(length)
    taps = normal_rows(filter_taps, place, epochs, length * epochs)
    tile = jnp.zeros((8, 128), jnp.float32)

    def summed(partial):
        return add_up(lax.all_gather(partial, "param", axis=0))

    def multiplied(blocks, tile):
        slots = multiply(high, low, taps, blocks, places, shards, tile)
        tile, *slots = lax.optimization_barrier((tile, *slots))
        return Reduction(slots, length), tile

    if chunks == 1 or length != 4:
        high, low, tall_high, tall_low = split_design(design, [taps, shards, places, tile])
        totals = []
        for chunk in range(chunks):
            gather = Gather(own[chunk * rows : (chunk + 1) * rows], length)
            for step in range(1, length):
                gather.send(0, step)
                gather.send(1, step)
            partial = project(tall_high, tall_low, own, chunk, gather.slots(), shards, tile)
            reduction, tile = multiplied(exchange(summed(partial), length), tile)
            for step in range(length - 1, 0, -1):
                reduction.send(0, step)
                reduction.send(1, step)
            totals.append(reduction.addends())
        return totals_of(totals, tile).T

    first = Gather(own[:rows], length)
    first.send(1, 1)
    first.send(0, 1)
    tile, taps, shards, places = lax.optimization_barrier((tile, taps, shards, places))
    tile = first.tie(tile, 0, 1)
    tile = first.tie(tile, 1, 1)
    first.send(0, 2)
    first.send(1, 2)
    tile = first.tie(tile, 1, 2)
    first.send(0, 3)
    high, low, tall_high, tall_low = split_design(design, [taps, shards, places, mark(tile)])
    tile, high, low, value = lax.optimization_barrier((tile, high, low, own[rows:]))
    second = Gather(value, length)
    second.send(0, 1)
    second.send(1, 1)
    partial = project(tall_high, tall_low, own, 0, first.slots(), shards, tile)
    projected = summed(partial)
    blocks = exchange(projected, length)
    tile, *blocks = lax.optimization_barrier((tile, *blocks))
    tile = second.tie(tile, 0, 1)
    tile = second.tie(tile, 1, 1)
    second.send(0, 2)
    second.send(1, 2)
    ahead, tile = multiplied(blocks, mark(tile))
    ahead.send(0, 3)
    ahead.send(0, 1, (True,))
    tile = second.tie(tile, 0, 2)
    tile = second.tie(tile, 1, 2)
    second.send(0, 3)
    tile = ahead.tie(mark(tile), 0, 3)
    ahead.send(0, 2)
    ahead.send(1, 2)
    partial = project(tall_high, tall_low, own, 1, second.slots(), shards, mark(tile))
    projected = summed(partial)
    blocks = exchange(projected, length)
    tile = ahead.tie(mark(tile, projected), 0, 2)
    tile = ahead.tie(tile, 1, 2)
    ahead.send(0, 1, (False,))
    ahead.send(1, 1)
    free = ahead.pending[0, 1][:1]
    tile, *free = lax.optimization_barrier((tile, *free))
    ahead.pending[0, 1][:1] = free
    trailing, tile = multiplied(blocks, mark(tile))
    trailing.send(0, 3)
    tile = ahead.tie(mark(tile), 0, 1)
    tile = ahead.tie(tile, 1, 1)
    tile, later = lax.optimization_barrier((tile, trailing.slots[2]))
    tile = mark(tile)
    tile = trailing.tie(tile, 0, 3)
    trailing.send(1, 2)
    trailing.slots[2] = later
    trailing.send(0, 2)
    trailing.send(0, 1)
    trailing.send(1, 1)
    return totals_of([ahead.addends(), trailing.addends()], tile).T


def solution(mesh):
    in_specs = (P(None, ("groups", "tm"), "param"), P(), P("param", ("groups", "tm")))
    out_specs = P("param", ("groups", "tm"))
    return jax.shard_map(body, mesh=mesh, in_specs=in_specs, out_specs=out_specs, check_vma=False)
```

```python
import math

import jax
import jax.numpy as jnp
from jax import lax
from jax.experimental import pallas as pl
from jax.experimental.pallas import tpu as pltpu
from jax.sharding import PartitionSpec as P


def cost(size):
    return pl.CostEstimate(flops=1, bytes_accessed=size, transcendentals=0)


SHORT = cost(1)
LONG = cost(200_000_000)
HIGHEST = lax.Precision.HIGHEST
ALONG = (((1,), (1,)), ((), ()))
ACROSS = (((1,), (0,)), ((), ()))


def split(value):
    high = value.astype(jnp.bfloat16)
    return high, (value - high.astype(jnp.float32)).astype(jnp.bfloat16)


def three_passes(left, right_high, right_low, dimensions=ACROSS):
    left_high, left_low = split(left)
    height = left.shape[0]
    both = jnp.concatenate([left_high, left_low], axis=0)
    first = lax.dot_general(both, right_high, dimensions, preferred_element_type=jnp.float32)
    last = lax.dot_general(left_high, right_low, dimensions, preferred_element_type=jnp.float32)
    return first[:height] + (first[height:] + last)


def split_design(design, earlier):
    components, epochs, coefficients = design.shape
    samples = components * epochs
    width = math.gcd(coefficients, 2048)

    def kernel(design_ref, *refs):
        high_ref, low_ref, tall_high_ref, tall_low_ref = refs[-4:]
        block = design_ref[...].reshape(samples, width)
        high_ref[...], low_ref[...] = split(block)
        tall_high_ref[...], tall_low_ref[...] = split(block.T)

    flat = jax.ShapeDtypeStruct((samples, coefficients), jnp.bfloat16)
    tall = jax.ShapeDtypeStruct((coefficients, samples), jnp.bfloat16)
    return pl.pallas_call(
        kernel,
        grid=(coefficients // width,),
        in_specs=[pl.BlockSpec((components, epochs, width), lambda p: (0, 0, p))]
        + [pl.BlockSpec(memory_space=pl.ANY)] * len(earlier),
        out_specs=[pl.BlockSpec((samples, width), lambda p: (0, p))] * 2
        + [pl.BlockSpec((width, samples), lambda p: (p, 0))] * 2,
        out_shape=[flat, flat, tall, tall],
        compiler_params=pltpu.CompilerParams(vmem_limit_bytes=16 << 20),
        cost_estimate=SHORT,
        name="split_design",
    )(design, *earlier)


def normal_rows(filter_taps, block_index, epochs, total):
    components, tap_count = filter_taps.shape
    lanes = -(-(total + tap_count) // 128) * 128

    def kernel(index_ref, taps_ref, out_ref, lag_ref):
        for c in range(components):
            row = jnp.concatenate([taps_ref[c : c + 1], jnp.zeros((1, lanes - tap_count), jnp.float32)], axis=1)
            square = jnp.broadcast_to(row, (epochs, lanes))
            for block in range(total // epochs):
                rolled = pltpu.roll(square, block * epochs, 1, stride=1, stride_axis=0)
                lag_ref[block * epochs : (block + 1) * epochs, :] = rolled[:, :total]
            staggered = pltpu.roll(square, 0, 1, stride=1, stride_axis=0)
            weight = pltpu.roll(staggered, index_ref[0] * epochs, 1)[:, :total]
            rows = lax.dot_general(weight, lag_ref[...], ALONG, precision=HIGHEST, preferred_element_type=jnp.float32)
            for block in range(total // epochs):
                out_ref[block, c] = rows[:, block * epochs : (block + 1) * epochs]

    return pl.pallas_call(
        kernel,
        grid_spec=pltpu.PrefetchScalarGridSpec(
            num_scalar_prefetch=1,
            grid=(1,),
            in_specs=[pl.BlockSpec((components, tap_count), lambda c, index: (0, 0))],
            out_specs=pl.BlockSpec((total // epochs, components, epochs, epochs), lambda c, index: (0, 0, 0, 0)),
            scratch_shapes=[pltpu.VMEM((total, total), jnp.float32)],
        ),
        out_shape=jax.ShapeDtypeStruct((total // epochs, components, epochs, epochs), jnp.float32),
        compiler_params=pltpu.CompilerParams(vmem_limit_bytes=(8 << 20) + 6 * total * total),
        cost_estimate=SHORT,
        name="normal_rows",
    )(jnp.reshape(block_index, (1,)).astype(jnp.int32), filter_taps)


def project(tall_high, tall_low, own, chunk, arrivals, shards, tile):
    coefficients, samples = tall_high.shape
    slots = len(arrivals) + 1
    rows = arrivals[0][0].shape[0]
    width = math.gcd(coefficients, 10240)
    counts = [len(pieces) for pieces in arrivals]
    pieces = [piece for group in arrivals for piece in group]

    def kernel(shard_ref, high_ref, low_ref, own_ref, *refs):
        *piece_refs, _, out_ref = refs
        values = [own_ref[...]]
        start = 0
        for count in counts:
            value = piece_refs[start][...]
            for ref in piece_refs[start + 1 : start + count]:
                value = value + ref[...]
            values.append(value)
            start += count
        part = three_passes(jnp.concatenate(values, axis=0), high_ref[...], low_ref[...])

        @pl.when(pl.program_id(0) == 0)
        def _():
            out_ref[...] = jnp.zeros_like(out_ref)

        for slot in range(slots):
            out_ref[shard_ref[slot]] += part[slot * rows : (slot + 1) * rows]

    return pl.pallas_call(
        kernel,
        grid_spec=pltpu.PrefetchScalarGridSpec(
            num_scalar_prefetch=1,
            grid=(coefficients // width,),
            in_specs=[
                pl.BlockSpec((width, samples), lambda p, shard: (p, 0)),
                pl.BlockSpec((width, samples), lambda p, shard: (p, 0)),
                pl.BlockSpec((rows, width), lambda p, shard: (chunk, p)),
            ]
            + [pl.BlockSpec((rows, width), lambda p, shard: (0, p)) for _ in pieces]
            + [pl.BlockSpec(memory_space=pl.ANY)],
            out_specs=pl.BlockSpec((slots, rows, samples), lambda p, shard: (0, 0, 0)),
        ),
        out_shape=jax.ShapeDtypeStruct((slots, rows, samples), jnp.float32),
        compiler_params=pltpu.CompilerParams(vmem_limit_bytes=24 << 20),
        cost_estimate=SHORT,
        name="project",
    )(shards, tall_high, tall_low, own, *pieces, tile)


def multiply(high, low, taps, blocks, places, shards, tile):
    samples, coefficients = high.shape
    _, components, epochs, _ = taps.shape
    slots, rows, _ = blocks[0].shape
    width = math.gcd(coefficients, 10240)
    count = len(blocks)

    def kernel(shard_ref, place_ref, high_ref, low_ref, taps_ref, *refs):
        block_refs = refs[:count]
        out_refs = refs[count + 1 : -1]
        weighted_ref = refs[-1]

        @pl.when(pl.program_id(0) == 0)
        def _():
            sums = [0.0] * components
            for source in range(count):
                block = block_refs[source][...].reshape(slots * rows, samples)
                for c in range(components):
                    piece = block[:, c * epochs : (c + 1) * epochs]
                    factor = taps_ref[place_ref[source], c]
                    sums[c] = sums[c] + three_passes(piece, *split(factor), ALONG)
            weighted_ref[...] = jnp.concatenate(sums, axis=1).reshape(slots, rows, samples)

        weighted = jnp.concatenate([weighted_ref[shard_ref[slot]] for slot in range(slots)], axis=0)
        product = three_passes(weighted, high_ref[...], low_ref[...])
        for slot in range(slots):
            out_refs[slot][...] = product[slot * rows : (slot + 1) * rows]

    return pl.pallas_call(
        kernel,
        grid_spec=pltpu.PrefetchScalarGridSpec(
            num_scalar_prefetch=2,
            grid=(coefficients // width,),
            in_specs=[
                pl.BlockSpec((samples, width), lambda p, shard, place: (0, p)),
                pl.BlockSpec((samples, width), lambda p, shard, place: (0, p)),
                pl.BlockSpec(taps.shape, lambda p, shard, place: (0, 0, 0, 0)),
            ]
            + [pl.BlockSpec((slots, rows, samples), lambda p, shard, place: (0, 0, 0)) for _ in blocks]
            + [pl.BlockSpec(memory_space=pl.ANY)],
            out_specs=[pl.BlockSpec((rows, width), lambda p, shard, place: (0, p)) for _ in range(slots)],
            scratch_shapes=[pltpu.VMEM((slots, rows, samples), jnp.float32)],
        ),
        out_shape=[jax.ShapeDtypeStruct((rows, coefficients), jnp.float32) for _ in range(slots)],
        compiler_params=pltpu.CompilerParams(vmem_limit_bytes=24 << 20),
        cost_estimate=SHORT,
        name="multiply",
    )(shards, places, high, low, taps, *blocks, tile)


def add_up(shares):
    count, slots, rows, samples = shares.shape

    def kernel(shares_ref, out_ref):
        value = shares_ref[0]
        for share in range(1, count):
            value = value + shares_ref[share]
        out_ref[...] = value

    return pl.pallas_call(
        kernel,
        out_shape=jax.ShapeDtypeStruct((slots, rows, samples), jnp.float32),
        compiler_params=pltpu.CompilerParams(vmem_limit_bytes=8 << 20),
        cost_estimate=SHORT,
        name="add_up",
    )(shares)


def totals_of(groups, tile):
    rows, coefficients = groups[0][0].shape
    width = math.gcd(coefficients, 2560)
    values = [value for group in groups for value in group]

    def kernel(*refs):
        start = 0
        for index, group in enumerate(groups):
            value = refs[start][...]
            for ref in refs[start + 1 : start + len(group)]:
                value = value + ref[...]
            refs[-1][index * rows : (index + 1) * rows, :] = value
            start += len(group)

    return pl.pallas_call(
        kernel,
        grid=(coefficients // width,),
        in_specs=[pl.BlockSpec((rows, width), lambda p: (0, p)) for _ in values] + [pl.BlockSpec(memory_space=pl.ANY)],
        out_specs=pl.BlockSpec((rows * len(groups), width), lambda p: (0, p)),
        out_shape=jax.ShapeDtypeStruct((rows * len(groups), coefficients), jnp.float32),
        compiler_params=pltpu.CompilerParams(vmem_limit_bytes=12 << 20),
        cost_estimate=LONG,
        name="totals_of",
    )(*values, tile)


def step_pairs(length, step, parity):
    pairs = []
    for low in range(parity, length - 1, 2):
        if low - step + 1 >= 0:
            pairs.append((low, low + 1))
        if low + step < length:
            pairs.append((low + 1, low))
    return pairs


def mark(tile, *values):
    count = len(values)

    def kernel(tile_ref, *refs):
        refs[count][...] = tile_ref[...]

    return pl.pallas_call(
        kernel,
        in_specs=[pl.BlockSpec(memory_space=pltpu.VMEM)] + [pl.BlockSpec(memory_space=pl.ANY)] * count,
        out_shape=jax.ShapeDtypeStruct(tile.shape, tile.dtype),
        compiler_params=pltpu.CompilerParams(vmem_limit_bytes=1 << 20),
        cost_estimate=LONG,
        name="mark",
    )(tile, *values)


class Gather:
    def __init__(self, value, length):
        self.length = length
        self.onward = {(0, 0): value, (1, 0): value}
        self.arrived = {}

    def pairs(self, parity, step, onward):
        sources = {source for source, _ in step_pairs(self.length, step + 1, 1 - parity)}
        return [pair for pair in step_pairs(self.length, step, parity) if (pair[1] in sources) == onward]

    def send(self, parity, step, kinds=(True, False)):
        pairs = [pair for onward in kinds for pair in self.pairs(parity, step, onward)]
        if pairs:
            value = lax.ppermute(self.onward[1 - parity, step - 1], "tm", pairs)
            self.arrived.setdefault((parity, step), []).append(value)
            if True in kinds:
                self.onward[parity, step] = value

    def tie(self, tile, parity, step):
        values = self.arrived.get((parity, step), [])
        if values:
            places = [index for index, value in enumerate(values) if value is self.onward.get((parity, step))]
            tile, *values = lax.optimization_barrier((tile, *values))
            self.arrived[parity, step] = values
            for index in places:
                self.onward[parity, step] = values[index]
        return tile

    def slots(self):
        return [
            self.arrived.get((0, slot), []) + self.arrived.get((1, self.length - slot), [])
            for slot in range(1, self.length)
        ]


class Reduction:
    def __init__(self, slots, length):
        self.length = length
        self.slots = slots
        self.pending = {}

    def pairs(self, parity, step, free):
        receivers = {source for source, _ in step_pairs(self.length, step + 1, 1 - parity)}
        pairs = [(b, a) for a, b in step_pairs(self.length, step, parity)]
        return [pair for pair in pairs if (pair[0] not in receivers) == free]

    def send(self, parity, step, kinds=(True, False)):
        pairs = [pair for free in kinds for pair in self.pairs(parity, step, free)]
        if pairs:
            value = self.slots[step] if parity == 0 else self.slots[self.length - step]
            if False in kinds:
                for other in self.pending.get((1 - parity, step + 1), []):
                    value = value + other
            self.pending.setdefault((parity, step), []).append(lax.ppermute(value, "tm", pairs))

    def tie(self, tile, parity, step):
        values = self.pending.get((parity, step), [])
        if values:
            tile, *values = lax.optimization_barrier((tile, *values))
            self.pending[parity, step] = values
        return tile

    def addends(self):
        return [self.slots[0]] + self.pending.get((0, 1), []) + self.pending.get((1, 1), [])


def is_direct(length):
    return length <= 8 and length & (length - 1) == 0


def places_of(length):
    numbers = jnp.arange(length, dtype=jnp.int32)
    return lax.axis_index("tm") ^ numbers if is_direct(length) else numbers


def exchange(value, length):
    if is_direct(length):
        return [value] + [lax.ppermute(value, "tm", [(i, i ^ by) for i in range(length)]) for by in range(1, length)]
    gathered = lax.all_gather(value, "tm", axis=0)
    return [gathered[i] for i in range(length)]


def body(design, filter_taps, probes):
    components, epochs, coefficients = design.shape
    length = lax.axis_size("tm")
    place = lax.axis_index("tm")
    own = probes.T
    columns = own.shape[0]
    chunks = 2 if columns % 16 == 0 else 1
    rows = columns // chunks
    direction = 1 - 2 * (place % 2)
    shards = (place + direction * jnp.arange(length, dtype=jnp.int32)) % length
    places = places_of(length)
    taps = normal_rows(filter_taps, place, epochs, length * epochs)
    tile = jnp.zeros((8, 128), jnp.float32)

    def summed(partial):
        return add_up(lax.all_gather(partial, "param", axis=0))

    def multiplied(blocks, tile):
        slots = multiply(high, low, taps, blocks, places, shards, tile)
        tile, *slots = lax.optimization_barrier((tile, *slots))
        return Reduction(slots, length), tile

    if chunks == 1 or length != 4:
        high, low, tall_high, tall_low = split_design(design, [taps, shards, places, tile])
        totals = []
        for chunk in range(chunks):
            gather = Gather(own[chunk * rows : (chunk + 1) * rows], length)
            for step in range(1, length):
                gather.send(0, step)
                gather.send(1, step)
            partial = project(tall_high, tall_low, own, chunk, gather.slots(), shards, tile)
            reduction, tile = multiplied(exchange(summed(partial), length), tile)
            for step in range(length - 1, 0, -1):
                reduction.send(0, step)
                reduction.send(1, step)
            totals.append(reduction.addends())
        return totals_of(totals, tile).T

    first = Gather(own[:rows], length)
    first.send(1, 1)
    first.send(0, 1)
    tile, taps, shards, places = lax.optimization_barrier((tile, taps, shards, places))
    tile = first.tie(tile, 0, 1)
    tile = first.tie(tile, 1, 1)
    first.send(0, 2)
    first.send(1, 2)
    tile = first.tie(tile, 1, 2)
    first.send(0, 3)
    high, low, tall_high, tall_low = split_design(design, [taps, shards, places, mark(tile)])
    tile, high, low, held = lax.optimization_barrier((tile, high, low, own))
    value = held[rows:]
    second = Gather(value, length)
    second.send(0, 1)
    second.send(1, 1)
    partial = project(tall_high, tall_low, own, 0, first.slots(), shards, tile)
    projected = summed(partial)
    blocks = exchange(projected, length)
    tile, *blocks = lax.optimization_barrier((tile, *blocks))
    tile = second.tie(tile, 0, 1)
    tile = second.tie(tile, 1, 1)
    second.send(0, 2)
    second.send(1, 2)
    ahead, tile = multiplied(blocks, mark(tile))
    ahead.send(0, 3)
    ahead.send(0, 1, (True,))
    tile = second.tie(tile, 0, 2)
    tile = second.tie(tile, 1, 2)
    second.send(0, 3)
    tile = ahead.tie(mark(tile), 0, 3)
    ahead.send(0, 2)
    ahead.send(1, 2)
    partial = project(tall_high, tall_low, own, 1, second.slots(), shards, mark(tile))
    projected = summed(partial)
    blocks = exchange(projected, length)
    tile = ahead.tie(mark(tile, projected), 0, 2)
    tile = ahead.tie(tile, 1, 2)
    ahead.send(0, 1, (False,))
    ahead.send(1, 1)
    free = ahead.pending[0, 1][:1]
    tile, *free = lax.optimization_barrier((tile, *free))
    ahead.pending[0, 1][:1] = free
    trailing, tile = multiplied(blocks, mark(tile))
    trailing.send(0, 3)
    tile = ahead.tie(mark(tile), 0, 1)
    tile = ahead.tie(tile, 1, 1)
    tile, later = lax.optimization_barrier((tile, trailing.slots[2]))
    tile = mark(tile)
    tile = trailing.tie(tile, 0, 3)
    trailing.send(1, 2)
    trailing.slots[2] = later
    trailing.send(0, 2)
    trailing.send(0, 1)
    trailing.send(1, 1)
    return totals_of([ahead.addends(), trailing.addends()], tile).T


def solution(mesh):
    in_specs = (P(None, ("groups", "tm"), "param"), P(), P("param", ("groups", "tm")))
    out_specs = P("param", ("groups", "tm"))
    return jax.shard_map(body, mesh=mesh, in_specs=in_specs, out_specs=out_specs, check_vma=False)
```

```python
import math

import jax
import jax.numpy as jnp
from jax import lax
from jax.experimental import pallas as pl
from jax.experimental.pallas import tpu as pltpu
from jax.sharding import PartitionSpec as P


def cost(size):
    return pl.CostEstimate(flops=1, bytes_accessed=size, transcendentals=0)


SHORT = cost(1)
LONG = cost(200_000_000)
HIGHEST = lax.Precision.HIGHEST
ALONG = (((1,), (1,)), ((), ()))
ACROSS = (((1,), (0,)), ((), ()))


def split(value):
    high = value.astype(jnp.bfloat16)
    return high, (value - high.astype(jnp.float32)).astype(jnp.bfloat16)


def three_passes(left, right_high, right_low, dimensions=ACROSS):
    left_high, left_low = split(left)
    height = left.shape[0]
    both = jnp.concatenate([left_high, left_low], axis=0)
    first = lax.dot_general(both, right_high, dimensions, preferred_element_type=jnp.float32)
    last = lax.dot_general(left_high, right_low, dimensions, preferred_element_type=jnp.float32)
    return first[:height] + (first[height:] + last)


def split_design(design, earlier):
    components, epochs, coefficients = design.shape
    samples = components * epochs
    width = math.gcd(coefficients, 2048)

    def kernel(design_ref, *refs):
        high_ref, low_ref, tall_high_ref, tall_low_ref = refs[-4:]
        block = design_ref[...].reshape(samples, width)
        high_ref[...], low_ref[...] = split(block)
        tall_high_ref[...], tall_low_ref[...] = split(block.T)

    flat = jax.ShapeDtypeStruct((samples, coefficients), jnp.bfloat16)
    tall = jax.ShapeDtypeStruct((coefficients, samples), jnp.bfloat16)
    return pl.pallas_call(
        kernel,
        grid=(coefficients // width,),
        in_specs=[pl.BlockSpec((components, epochs, width), lambda p: (0, 0, p))]
        + [pl.BlockSpec(memory_space=pl.ANY)] * len(earlier),
        out_specs=[pl.BlockSpec((samples, width), lambda p: (0, p))] * 2
        + [pl.BlockSpec((width, samples), lambda p: (p, 0))] * 2,
        out_shape=[flat, flat, tall, tall],
        compiler_params=pltpu.CompilerParams(vmem_limit_bytes=16 << 20),
        cost_estimate=SHORT,
        name="split_design",
    )(design, *earlier)


def normal_rows(filter_taps, block_index, epochs, total):
    components, tap_count = filter_taps.shape
    lanes = -(-(total + tap_count) // 128) * 128

    def kernel(index_ref, taps_ref, out_ref, lag_ref):
        for c in range(components):
            row = jnp.concatenate([taps_ref[c : c + 1], jnp.zeros((1, lanes - tap_count), jnp.float32)], axis=1)
            square = jnp.broadcast_to(row, (epochs, lanes))
            for block in range(total // epochs):
                rolled = pltpu.roll(square, block * epochs, 1, stride=1, stride_axis=0)
                lag_ref[block * epochs : (block + 1) * epochs, :] = rolled[:, :total]
            staggered = pltpu.roll(square, 0, 1, stride=1, stride_axis=0)
            weight = pltpu.roll(staggered, index_ref[0] * epochs, 1)[:, :total]
            rows = lax.dot_general(weight, lag_ref[...], ALONG, precision=HIGHEST, preferred_element_type=jnp.float32)
            for block in range(total // epochs):
                out_ref[block, c] = rows[:, block * epochs : (block + 1) * epochs]

    return pl.pallas_call(
        kernel,
        grid_spec=pltpu.PrefetchScalarGridSpec(
            num_scalar_prefetch=1,
            grid=(1,),
            in_specs=[pl.BlockSpec((components, tap_count), lambda c, index: (0, 0))],
            out_specs=pl.BlockSpec((total // epochs, components, epochs, epochs), lambda c, index: (0, 0, 0, 0)),
            scratch_shapes=[pltpu.VMEM((total, total), jnp.float32)],
        ),
        out_shape=jax.ShapeDtypeStruct((total // epochs, components, epochs, epochs), jnp.float32),
        compiler_params=pltpu.CompilerParams(vmem_limit_bytes=(8 << 20) + 6 * total * total),
        cost_estimate=SHORT,
        name="normal_rows",
    )(jnp.reshape(block_index, (1,)).astype(jnp.int32), filter_taps)


def project(tall_high, tall_low, own, chunk, arrivals, shards, tile):
    coefficients, samples = tall_high.shape
    slots = len(arrivals) + 1
    rows = arrivals[0][0].shape[0]
    width = math.gcd(coefficients, 10240)
    counts = [len(pieces) for pieces in arrivals]
    pieces = [piece for group in arrivals for piece in group]

    def kernel(shard_ref, high_ref, low_ref, own_ref, *refs):
        *piece_refs, _, out_ref = refs
        values = [own_ref[...]]
        start = 0
        for count in counts:
            value = piece_refs[start][...]
            for ref in piece_refs[start + 1 : start + count]:
                value = value + ref[...]
            values.append(value)
            start += count
        part = three_passes(jnp.concatenate(values, axis=0), high_ref[...], low_ref[...])

        @pl.when(pl.program_id(0) == 0)
        def _():
            out_ref[...] = jnp.zeros_like(out_ref)

        for slot in range(slots):
            out_ref[shard_ref[slot]] += part[slot * rows : (slot + 1) * rows]

    return pl.pallas_call(
        kernel,
        grid_spec=pltpu.PrefetchScalarGridSpec(
            num_scalar_prefetch=1,
            grid=(coefficients // width,),
            in_specs=[
                pl.BlockSpec((width, samples), lambda p, shard: (p, 0)),
                pl.BlockSpec((width, samples), lambda p, shard: (p, 0)),
                pl.BlockSpec((rows, width), lambda p, shard: (chunk, p)),
            ]
            + [pl.BlockSpec((rows, width), lambda p, shard: (0, p)) for _ in pieces]
            + [pl.BlockSpec(memory_space=pl.ANY)],
            out_specs=pl.BlockSpec((slots, rows, samples), lambda p, shard: (0, 0, 0)),
        ),
        out_shape=jax.ShapeDtypeStruct((slots, rows, samples), jnp.float32),
        compiler_params=pltpu.CompilerParams(vmem_limit_bytes=24 << 20),
        cost_estimate=SHORT,
        name="project",
    )(shards, tall_high, tall_low, own, *pieces, tile)


def multiply(high, low, taps, blocks, places, shards, tile):
    samples, coefficients = high.shape
    _, components, epochs, _ = taps.shape
    slots, rows, _ = blocks[0].shape
    width = math.gcd(coefficients, 10240)
    count = len(blocks)

    def kernel(shard_ref, place_ref, high_ref, low_ref, taps_ref, *refs):
        block_refs = refs[:count]
        out_refs = refs[count + 1 : -1]
        weighted_ref = refs[-1]

        @pl.when(pl.program_id(0) == 0)
        def _():
            sums = [0.0] * components
            for source in range(count):
                block = block_refs[source][...].reshape(slots * rows, samples)
                for c in range(components):
                    piece = block[:, c * epochs : (c + 1) * epochs]
                    factor = taps_ref[place_ref[source], c]
                    sums[c] = sums[c] + three_passes(piece, *split(factor), ALONG)
            weighted_ref[...] = jnp.concatenate(sums, axis=1).reshape(slots, rows, samples)

        weighted = jnp.concatenate([weighted_ref[shard_ref[slot]] for slot in range(slots)], axis=0)
        product = three_passes(weighted, high_ref[...], low_ref[...])
        for slot in range(slots):
            out_refs[slot][...] = product[slot * rows : (slot + 1) * rows]

    return pl.pallas_call(
        kernel,
        grid_spec=pltpu.PrefetchScalarGridSpec(
            num_scalar_prefetch=2,
            grid=(coefficients // width,),
            in_specs=[
                pl.BlockSpec((samples, width), lambda p, shard, place: (0, p)),
                pl.BlockSpec((samples, width), lambda p, shard, place: (0, p)),
                pl.BlockSpec(taps.shape, lambda p, shard, place: (0, 0, 0, 0)),
            ]
            + [pl.BlockSpec((slots, rows, samples), lambda p, shard, place: (0, 0, 0)) for _ in blocks]
            + [pl.BlockSpec(memory_space=pl.ANY)],
            out_specs=[pl.BlockSpec((rows, width), lambda p, shard, place: (0, p)) for _ in range(slots)],
            scratch_shapes=[pltpu.VMEM((slots, rows, samples), jnp.float32)],
        ),
        out_shape=[jax.ShapeDtypeStruct((rows, coefficients), jnp.float32) for _ in range(slots)],
        compiler_params=pltpu.CompilerParams(vmem_limit_bytes=24 << 20),
        cost_estimate=SHORT,
        name="multiply",
    )(shards, places, high, low, taps, *blocks, tile)


def add_up(shares):
    count, slots, rows, samples = shares.shape

    def kernel(shares_ref, out_ref):
        value = shares_ref[0]
        for share in range(1, count):
            value = value + shares_ref[share]
        out_ref[...] = value

    return pl.pallas_call(
        kernel,
        out_shape=jax.ShapeDtypeStruct((slots, rows, samples), jnp.float32),
        compiler_params=pltpu.CompilerParams(vmem_limit_bytes=8 << 20),
        cost_estimate=SHORT,
        name="add_up",
    )(shares)


def totals_of(groups, tile):
    rows, coefficients = groups[0][0].shape
    width = math.gcd(coefficients, 5120)
    values = [value for group in groups for value in group]

    def kernel(*refs):
        start = 0
        for index, group in enumerate(groups):
            value = refs[start][...]
            for ref in refs[start + 1 : start + len(group)]:
                value = value + ref[...]
            refs[-1][index * rows : (index + 1) * rows, :] = value
            start += len(group)

    return pl.pallas_call(
        kernel,
        grid=(coefficients // width,),
        in_specs=[pl.BlockSpec((rows, width), lambda p: (0, p)) for _ in values] + [pl.BlockSpec(memory_space=pl.ANY)],
        out_specs=pl.BlockSpec((rows * len(groups), width), lambda p: (0, p)),
        out_shape=jax.ShapeDtypeStruct((rows * len(groups), coefficients), jnp.float32),
        compiler_params=pltpu.CompilerParams(vmem_limit_bytes=12 << 20),
        cost_estimate=LONG,
        name="totals_of",
    )(*values, tile)


def step_pairs(length, step, parity):
    pairs = []
    for low in range(parity, length - 1, 2):
        if low - step + 1 >= 0:
            pairs.append((low, low + 1))
        if low + step < length:
            pairs.append((low + 1, low))
    return pairs


def mark(tile, *values):
    count = len(values)

    def kernel(tile_ref, *refs):
        refs[count][...] = tile_ref[...]

    return pl.pallas_call(
        kernel,
        in_specs=[pl.BlockSpec(memory_space=pltpu.VMEM)] + [pl.BlockSpec(memory_space=pl.ANY)] * count,
        out_shape=jax.ShapeDtypeStruct(tile.shape, tile.dtype),
        compiler_params=pltpu.CompilerParams(vmem_limit_bytes=1 << 20),
        cost_estimate=LONG,
        name="mark",
    )(tile, *values)


class Gather:
    def __init__(self, value, length):
        self.length = length
        self.onward = {(0, 0): value, (1, 0): value}
        self.arrived = {}

    def pairs(self, parity, step, onward):
        sources = {source for source, _ in step_pairs(self.length, step + 1, 1 - parity)}
        return [pair for pair in step_pairs(self.length, step, parity) if (pair[1] in sources) == onward]

    def send(self, parity, step, kinds=(True, False)):
        pairs = [pair for onward in kinds for pair in self.pairs(parity, step, onward)]
        if pairs:
            value = lax.ppermute(self.onward[1 - parity, step - 1], "tm", pairs)
            self.arrived.setdefault((parity, step), []).append(value)
            if True in kinds:
                self.onward[parity, step] = value

    def tie(self, tile, parity, step):
        values = self.arrived.get((parity, step), [])
        if values:
            places = [index for index, value in enumerate(values) if value is self.onward.get((parity, step))]
            tile, *values = lax.optimization_barrier((tile, *values))
            self.arrived[parity, step] = values
            for index in places:
                self.onward[parity, step] = values[index]
        return tile

    def slots(self):
        return [
            self.arrived.get((0, slot), []) + self.arrived.get((1, self.length - slot), [])
            for slot in range(1, self.length)
        ]


class Reduction:
    def __init__(self, slots, length):
        self.length = length
        self.slots = slots
        self.pending = {}

    def pairs(self, parity, step, free):
        receivers = {source for source, _ in step_pairs(self.length, step + 1, 1 - parity)}
        pairs = [(b, a) for a, b in step_pairs(self.length, step, parity)]
        return [pair for pair in pairs if (pair[0] not in receivers) == free]

    def send(self, parity, step, kinds=(True, False)):
        pairs = [pair for free in kinds for pair in self.pairs(parity, step, free)]
        if pairs:
            value = self.slots[step] if parity == 0 else self.slots[self.length - step]
            if False in kinds:
                for other in self.pending.get((1 - parity, step + 1), []):
                    value = value + other
            self.pending.setdefault((parity, step), []).append(lax.ppermute(value, "tm", pairs))

    def tie(self, tile, parity, step):
        values = self.pending.get((parity, step), [])
        if values:
            tile, *values = lax.optimization_barrier((tile, *values))
            self.pending[parity, step] = values
        return tile

    def addends(self):
        return [self.slots[0]] + self.pending.get((0, 1), []) + self.pending.get((1, 1), [])


def is_direct(length):
    return length <= 8 and length & (length - 1) == 0


def places_of(length):
    numbers = jnp.arange(length, dtype=jnp.int32)
    return lax.axis_index("tm") ^ numbers if is_direct(length) else numbers


def exchange(value, length):
    if is_direct(length):
        others = [lax.ppermute(value, "tm", [(i, i ^ by) for i in range(length)]) for by in range(length - 1, 0, -1)]
        return [value] + others[::-1]
    gathered = lax.all_gather(value, "tm", axis=0)
    return [gathered[i] for i in range(length)]


def body(design, filter_taps, probes):
    components, epochs, coefficients = design.shape
    length = lax.axis_size("tm")
    place = lax.axis_index("tm")
    own = probes.T
    columns = own.shape[0]
    chunks = 2 if columns % 16 == 0 else 1
    rows = columns // chunks
    direction = 1 - 2 * (place % 2)
    shards = (place + direction * jnp.arange(length, dtype=jnp.int32)) % length
    places = places_of(length)
    taps = normal_rows(filter_taps, place, epochs, length * epochs)
    tile = jnp.zeros((8, 128), jnp.float32)

    def summed(partial):
        return add_up(lax.all_gather(partial, "param", axis=0))

    def multiplied(blocks, tile):
        slots = multiply(high, low, taps, blocks, places, shards, tile)
        tile, *slots = lax.optimization_barrier((tile, *slots))
        return Reduction(slots, length), tile

    if chunks == 1 or length != 4:
        high, low, tall_high, tall_low = split_design(design, [taps, shards, places, tile])
        totals = []
        for chunk in range(chunks):
            gather = Gather(own[chunk * rows : (chunk + 1) * rows], length)
            for step in range(1, length):
                gather.send(0, step)
                gather.send(1, step)
            partial = project(tall_high, tall_low, own, chunk, gather.slots(), shards, tile)
            reduction, tile = multiplied(exchange(summed(partial), length), tile)
            for step in range(length - 1, 0, -1):
                reduction.send(0, step)
                reduction.send(1, step)
            totals.append(reduction.addends())
        return totals_of(totals, tile).T

    first = Gather(own[:rows], length)
    first.send(1, 1)
    first.send(0, 1)
    tile, taps, shards, places = lax.optimization_barrier((tile, taps, shards, places))
    tile = first.tie(tile, 0, 1)
    tile = first.tie(tile, 1, 1)
    first.send(0, 2)
    first.send(1, 2)
    tile = first.tie(tile, 1, 2)
    first.send(0, 3)
    high, low, tall_high, tall_low = split_design(design, [taps, shards, places, mark(tile)])
    tile, high, low, value = lax.optimization_barrier((tile, high, low, own[rows:]))
    second = Gather(value, length)
    second.send(0, 1)
    second.send(1, 1)
    partial = project(tall_high, tall_low, own, 0, first.slots(), shards, tile)
    projected = summed(partial)
    blocks = exchange(projected, length)
    tile, *blocks = lax.optimization_barrier((tile, *blocks))
    tile = second.tie(tile, 0, 1)
    tile = second.tie(tile, 1, 1)
    second.send(0, 2)
    second.send(1, 2)
    ahead, tile = multiplied(blocks, mark(tile))
    ahead.send(0, 3)
    ahead.send(0, 1, (True,))
    tile = second.tie(tile, 0, 2)
    tile = second.tie(tile, 1, 2)
    second.send(0, 3)
    tile = ahead.tie(mark(tile), 0, 3)
    ahead.send(0, 2)
    ahead.send(1, 2)
    partial = project(tall_high, tall_low, own, 1, second.slots(), shards, mark(tile))
    projected = summed(partial)
    blocks = exchange(projected, length)
    tile = ahead.tie(mark(tile, projected), 0, 2)
    tile = ahead.tie(tile, 1, 2)
    ahead.send(0, 1, (False,))
    ahead.send(1, 1)
    free = ahead.pending[0, 1][:1]
    tile, *free = lax.optimization_barrier((tile, *free))
    ahead.pending[0, 1][:1] = free
    trailing, tile = multiplied(blocks, mark(tile))
    trailing.send(0, 3)
    tile = ahead.tie(mark(tile), 0, 1)
    tile = ahead.tie(tile, 1, 1)
    tile, later = lax.optimization_barrier((tile, trailing.slots[2]))
    tile = mark(tile)
    tile = trailing.tie(tile, 0, 3)
    trailing.send(1, 2)
    trailing.slots[2] = later
    trailing.send(0, 2)
    trailing.send(0, 1)
    trailing.send(1, 1)
    return totals_of([ahead.addends(), trailing.addends()], tile).T


def solution(mesh):
    in_specs = (P(None, ("groups", "tm"), "param"), P(), P("param", ("groups", "tm")))
    out_specs = P("param", ("groups", "tm"))
    return jax.shard_map(body, mesh=mesh, in_specs=in_specs, out_specs=out_specs, check_vma=False)
```
